128 devices in a mesh: rep: 2 (over core), width: 8 (over y, x_lo), hid: 8 (over z, x_hi).
Axes of the slice: x: 4 (x_hi: 2, x_lo: 2; x = x_hi * 2 + x_lo), y: 4, z: 4, core: 2. Of those that a mesh axis runs over, the one named last changes fastest.
Arguments:
- tokens: float32 [256, 5120], P(('rep', 'hid'), 'width'), may hold values from -6 to 6
- cotangent: float32 [256, 5120], P(('rep', 'hid'), 'width'), may hold values from -6 to 6
- w_gate: float32 [5120, 6912], P('width', 'hid'), may hold values from -0.078125 to 0.078125
- w_up: float32 [5120, 6912], P('width', 'hid'), may hold values from -0.078125 to 0.078125
- w_down: float32 [6912, 5120], P('hid', 'width'), may hold values from -0.078125 to 0.078125
Outputs:
- output: float32 [256, 5120], P(('rep', 'hid'), 'width')
- grad_tokens: float32 [256, 5120], P(('rep', 'hid'), 'width')
- grad_gate: float32 [8, 2, 320, 6912], P('width', 'rep', None, 'hid')
- grad_up: float32 [8, 2, 320, 6912], P('width', 'rep', None, 'hid')
- grad_down: float32 [8, 2, 432, 5120], P('hid', 'rep', None, 'width')
The draws below stay inside these ranges and needn't reach their ends.
All inputs are finite; a program needn't handle non-finite values.
Results may differ from the reference program's by a relative error of at most 0.00016.
Values sent between devices are 32-bit elements; how exact they have to be, the bound alone decides.
A program may use at most 64 MiB of HBM per device.

```python
import jax
import jax.numpy as jnp
from jax import lax

D = 5120
FF = 6912
TOKENS = 256
N_WIDTH = 8
N_HID = 8


def level_of(own_key, shape, shards, smallest, high):
    loudness = 1.0
    for axis_at, parts in shards:
        draws = jax.random.uniform(jax.random.fold_in(jax.random.fold_in(own_key, 6), axis_at), (parts,), jnp.float32, smallest / len(shards), high / len(shards))
        loudness = loudness * jnp.repeat(jnp.exp(draws), shape[axis_at] // parts).reshape((-1,) + (1,) * (len(shape) - 1 - axis_at))
    return loudness


def centred(stream_key, shape, deviation, reach, shards=(), dtype=jnp.bfloat16):
    array = deviation * jax.random.normal(stream_key, shape, jnp.float32)
    if shards:
        array = array * level_of(stream_key, shape, shards, -0.22, 0.18)
    return jnp.clip(array, -reach, reach).astype(dtype)


def setup_inputs(seed: int = 0) -> dict:
    keys = jax.random.split(jax.random.key(seed), 6)
    tokens = centred(keys[0], (TOKENS, D), 1.0, 6.0, ((0, 16), (1, 8)), jnp.float32)
    cotangent = centred(keys[1], (TOKENS, D), 1.0, 6.0, ((0, 16), (1, 8)), jnp.float32)
    w_gate = centred(keys[2], (D, FF), D ** -0.5, 0.078125, ((0, 8), (1, 8)), jnp.float32)
    w_up = centred(keys[3], (D, FF), D ** -0.5, 0.078125, ((0, 8), (1, 8)), jnp.float32)
    w_down = centred(keys[4], (FF, D), FF ** -0.5, 0.078125, ((0, 8), (1, 8)), jnp.float32)
    return {"tokens": tokens, "cotangent": cotangent, "w_gate": w_gate, "w_up": w_up, "w_down": w_down}


def forward_dot(left, right):
    return jnp.dot(left, right, precision=lax.Precision.HIGHEST, preferred_element_type=jnp.float32)


def reference(tokens, cotangent, w_gate, w_up, w_down):
    gate = forward_dot(tokens, w_gate)
    up = forward_dot(tokens, w_up)
    logistic = jax.nn.sigmoid(gate)
    hidden = gate * logistic * up
    output = forward_dot(hidden, w_down)
    grad_hidden = forward_dot(cotangent, w_down.T)
    gate_grad = grad_hidden * up * logistic * (1.0 + gate * (1.0 - logistic))
    up_grad = grad_hidden * gate * logistic
    grad_tokens = forward_dot(gate_grad, w_gate.T) + forward_dot(up_grad, w_up.T)
    grad_gate = forward_dot(tokens.T, gate_grad).reshape(N_WIDTH, 2, D // (2 * N_WIDTH), FF)
    grad_up = forward_dot(tokens.T, up_grad).reshape(N_WIDTH, 2, D // (2 * N_WIDTH), FF)
    grad_down = forward_dot(hidden.T, cotangent).reshape(N_HID, 2, FF // (2 * N_HID), D)
    return output, grad_tokens, grad_gate, grad_up, grad_down
```

```python
import functools

import jax
import jax.numpy as jnp
from jax import lax
from jax.experimental import pallas as pl
from jax.experimental.pallas import tpu as pltpu
from jax.sharding import PartitionSpec as P

MESH = pl.DeviceIdType.MESH
F32 = jnp.float32
BF16 = jnp.bfloat16
NN = (((1,), (0,)), ((), ()))
NT = (((1,), (1,)), ((), ()))
ROWS = 128
W = 640
H = 864
HP = 896
X_OFFS = [(a, b) for a in range(4) for b in range(2) if (a, b) != (0, 0)]


def split(v):
    hi = v.astype(BF16)
    return hi, (v - hi.astype(F32)).astype(BF16)


def dot(a, b, dims):
    return lax.dot_general(a, b, dims, preferred_element_type=F32)


def dot3(stack, b_hi, b_lo, dims):
    m = stack.shape[0] // 2
    both = dot(stack, b_hi, dims)
    return both[:m] + both[m:] + dot(stack[:m], b_lo, dims)


def kernel(
    tok_in, cot_in, wg_in, wu_in, wd_in,
    out_o, gtok_o, gg_o, gu_o, gd_o,
    xf, df, xs, ds_, wgf, wuf, wdf, wgh, wgl, wuh, wul, wdh, wdl,
    part, r1, r2, r3, r4, s1, s3, own, full,
    xt, xt_far, dy_far, ht, ht_far, far,
    xth, xtl, hth, htl, bh, bl, dh, dl,
    op, gp, rg, o_own, g_own, wgrad, dgrad,
    a_s, a_r, c_s, c_r, e_s, e_r, g_s, g_r, p_s, p_r, l_s,
):
    rep = lax.axis_index("rep")
    w = lax.axis_index("width")
    h = lax.axis_index("hid")
    y, xl = w // 2, w % 2
    z, xh = h // 2, h % 2

    def ydev(k):
        return (rep, ((y + k) % 4) * 2 + xl, h)

    xdev = (rep, y * 2 + (1 - xl), h)

    def hdev(off):
        return (rep, w, ((z + off[0]) % 4) * 2 + (xh + off[1]) % 2)

    pdev = (1 - rep, w, h)
    sent = []

    def send(src, dst, s, r, device):
        c = pltpu.make_async_remote_copy(
            src_ref=src, dst_ref=dst, send_sem=s, recv_sem=r,
            device_id=device, device_id_type=MESH,
        )
        c.start()
        sent.append(c)
        return c

    def local(src, dst, i):
        c = pltpu.make_async_copy(src, dst, l_s.at[i])
        c.start()
        return c

    hrow = pl.multiple_of(h * 16, 16)
    lx = local(tok_in, xf.at[pl.ds(hrow, 16)], 0)
    ly = local(cot_in, df.at[pl.ds(hrow, 16)], 1)
    lg = local(wg_in, wgf, 2)
    lu = local(wu_in, wuf, 3)
    ld = local(wd_in, wdf, 4)

    barrier = pltpu.get_barrier_semaphore()
    peers = [ydev(k) for k in (1, 2, 3)] + [xdev] + [hdev(o) for o in X_OFFS] + [pdev]
    for d in peers:
        pl.semaphore_signal(barrier, inc=1, device_id=d, device_id_type=MESH)
    pl.semaphore_wait(barrier, len(peers))

    ax = [send(tok_in, xf.at[pl.ds(hrow, 16)], a_s.at[k], a_r.at[k], hdev(o)) for k, o in enumerate(X_OFFS)]
    ad = [send(cot_in, df.at[pl.ds(hrow, 16)], a_s.at[7 + k], a_r.at[7 + k], hdev(o)) for k, o in enumerate(X_OFFS)]

    def halves(src, hi_ref, lo_ref, rows, cols):
        step = 32

        def body(i, _):
            at = pl.multiple_of(i * step, step)
            hi, lo = split(src[pl.ds(at, step), :])
            hi_ref[pl.ds(at, step), pl.ds(0, cols)] = hi
            lo_ref[pl.ds(at, step), pl.ds(0, cols)] = lo
            return 0

        lax.fori_loop(0, rows // step, body, 0)

    for ref in (wgh, wgl, wuh, wul):
        ref[:, pl.ds(768, 128)] = jnp.zeros((W, 128), BF16)
    for ref in (wdh, wdl):
        ref[pl.ds(H, HP - H), :] = jnp.zeros((HP - H, W), BF16)
    lg.wait()
    halves(wgf, wgh, wgl, W, H)
    lu.wait()
    halves(wuf, wuh, wul, W, H)

    def scatter(a):
        c = [
            send(
                part.at[a, pl.ds(pl.multiple_of(32 * (1 - xl), 32), 32)], r1.at[a],
                c_s.at[a, 0], c_r.at[a, 0], xdev,
            )
        ]
        for k in (1, 2, 3):
            row = pl.multiple_of(64 + 16 * ((y + k) % 4), 16)
            c.append(
                send(part.at[a, pl.ds(row, 16)], r3.at[a, k - 1], c_s.at[a, k], c_r.at[a, k], ydev(k))
            )
        return c

    lx.wait()
    for c in ax:
        c.wait_recv()
    hi, lo = split(xf[...])
    xs[pl.ds(0, ROWS), :] = hi
    xs[pl.ds(ROWS, ROWS), :] = lo
    part[0] = dot3(xs[...], wgh[...], wgl[...], NN)
    c0 = scatter(0)
    part[1] = dot3(xs[...], wuh[...], wul[...], NN)
    c1 = scatter(1)
    ld.wait()
    halves(wdf, wdh, wdl, H, W)
    ly.wait()
    for c in ad:
        c.wait_recv()
    hi, lo = split(df[...])
    ds_[pl.ds(0, ROWS), :] = hi
    ds_[pl.ds(ROWS, ROWS), :] = lo
    part[2] = dot3(ds_[...], wdh[...], wdl[...], NT)
    c2 = scatter(2)
    p_dy = send(df, dy_far, p_s.at[0], p_r.at[0], pdev)

    def second(a, first):
        first[0].wait_recv()
        s1[a] = part[a, pl.ds(pl.multiple_of(32 * xl, 32), 32), :] + r1[a]
        c = []
        for k in (1, 2, 3):
            row = pl.multiple_of(8 * ((y + k) % 4), 8)
            c.append(
                send(s1.at[a, pl.ds(row, 8)], r2.at[a, k - 1], c_s.at[a, 3 + k], c_r.at[a, 3 + k], ydev(k))
            )
        for d in first[1:]:
            d.wait_recv()
        s3[a] = part[a, pl.ds(pl.multiple_of(64 + 16 * y, 16), 16), :] + r3[a, 0] + r3[a, 1] + r3[a, 2]
        c.append(
            send(
                s3.at[a, pl.ds(pl.multiple_of(8 * (1 - xl), 8), 8)], r4.at[a],
                c_s.at[a, 7], c_r.at[a, 7], xdev,
            )
        )
        return c

    def summed(a, c):
        for d in c:
            d.wait_recv()
        top = s1[a, pl.ds(pl.multiple_of(8 * y, 8), 8), :] + r2[a, 0] + r2[a, 1] + r2[a, 2]
        low = s3[a, pl.ds(pl.multiple_of(8 * xl, 8), 8), :] + r4[a]
        return jnp.concatenate([top, low], axis=0)

    top_row = pl.multiple_of(8 * (4 * xl + y), 8)
    low_row = pl.multiple_of(64 + 8 * (2 * y + xl), 8)
    low_pair = pl.multiple_of(64 + 16 * y, 16)
    top_half = pl.multiple_of(32 * xl, 32)

    def gather(a, value):
        full[a, pl.ds(top_row, 8), :] = value[:8]
        full[a, pl.ds(low_row, 8), :] = value[8:]
        c = [
            send(full.at[a, pl.ds(low_row, 8)], full.at[a, pl.ds(low_row, 8)], e_s.at[a, 0], e_r.at[a, 0], xdev)
        ]
        for k in (1, 2, 3):
            c.append(
                send(full.at[a, pl.ds(top_row, 8)], full.at[a, pl.ds(top_row, 8)], e_s.at[a, k], e_r.at[a, k], ydev(k))
            )
        return c

    def gather_on(a, first):
        first[0].wait_recv()
        c = []
        for k in (1, 2, 3):
            c.append(
                send(
                    full.at[a, pl.ds(low_pair, 16)], full.at[a, pl.ds(low_pair, 16)],
                    e_s.at[a, 3 + k], e_r.at[a, 3 + k], ydev(k),
                )
            )
        for d in first[1:]:
            d.wait_recv()
        c.append(
            send(
                full.at[a, pl.ds(top_half, 32)], full.at[a, pl.ds(top_half, 32)],
                e_s.at[a, 7], e_r.at[a, 7], xdev,
            )
        )
        return c

    d0 = second(0, c0)
    d1 = second(1, c1)
    d2 = second(2, c2)
    for j in range(5):
        xt[pl.ds(128 * j, 128), :] = xf[:, pl.ds(128 * j, 128)].T
    half_x = pl.multiple_of(320 * rep, 64)
    far_x = pl.multiple_of(320 * (1 - rep), 64)
    p_x = send(xt.at[pl.ds(far_x, 320)], xt_far, p_s.at[1], p_r.at[1], pdev)

    gate = summed(0, d0)
    up = summed(1, d1)
    logistic = 1.0 / (1.0 + jnp.exp(-gate))
    e0 = gather(0, gate * logistic * up)
    back = summed(2, d2)
    e1 = gather(1, back * up * logistic * (1.0 + gate * (1.0 - logistic)))
    e2 = gather(2, back * gate * logistic)

    f0 = gather_on(0, e0)
    f1 = gather_on(1, e1)
    f2 = gather_on(2, e2)

    def reduce_rows(src, i):
        c = []
        for k, o in enumerate(X_OFFS):
            row = pl.multiple_of(16 * (((z + o[0]) % 4) * 2 + (xh + o[1]) % 2), 16)
            c.append(send(src.at[pl.ds(row, 16)], rg.at[i, k], g_s.at[i, k], g_r.at[i, k], hdev(o)))
        return c

    for d in f0:
        d.wait_recv()
    hid = full[0]
    hi, lo = split(hid)
    op[...] = dot3(jnp.concatenate([hi, lo], axis=0), wdh[...], wdl[...], NN)
    g0 = reduce_rows(op, 0)
    for j in range(7):
        ht[pl.ds(128 * j, 128), :] = full[0, :, pl.ds(128 * j, 128)].T
    half_h = pl.multiple_of(432 * rep, 16)
    far_h = pl.multiple_of(432 * (1 - rep), 16)
    p_h = send(ht.at[pl.ds(far_h, 432)], ht_far, p_s.at[2], p_r.at[2], pdev)

    for d in f1:
        d.wait_recv()
    p_g = send(full.at[1], far.at[0], p_s.at[3], p_r.at[3], pdev)
    hi, lo = split(full[1])
    bh[0, pl.ds(0, ROWS), :] = hi
    bl[0, pl.ds(0, ROWS), :] = lo
    acc = dot3(jnp.concatenate([hi, lo], axis=0), wgh[...], wgl[...], NT)
    for d in f2:
        d.wait_recv()
    p_u = send(full.at[2], far.at[1], p_s.at[4], p_r.at[4], pdev)
    hi, lo = split(full[2])
    bh[1, pl.ds(0, ROWS), :] = hi
    bl[1, pl.ds(0, ROWS), :] = lo
    gp[...] = acc + dot3(jnp.concatenate([hi, lo], axis=0), wuh[...], wul[...], NT)
    g1 = reduce_rows(gp, 1)

    p_x.wait_recv()
    for ref, at in ((xt.at[pl.ds(half_x, 320)], 0), (xt_far, 128)):
        hi, lo = split(ref[...])
        xth[pl.ds(0, 320), pl.ds(at, 128)] = hi
        xth[pl.ds(320, 320), pl.ds(at, 128)] = lo
    p_dy.wait_recv()
    dh[pl.ds(0, ROWS), :] = ds_[pl.ds(0, ROWS), :]
    dl[pl.ds(0, ROWS), :] = ds_[pl.ds(ROWS, ROWS), :]
    hi, lo = split(dy_far[...])
    dh[pl.ds(ROWS, ROWS), :] = hi
    dl[pl.ds(ROWS, ROWS), :] = lo
    p_h.wait_recv()
    for ref, at in ((ht.at[pl.ds(half_h, 432)], 0), (ht_far, 128)):
        hi, lo = split(ref[...])
        hth[pl.ds(0, 432), pl.ds(at, 128)] = hi
        hth[pl.ds(432, 432), pl.ds(at, 128)] = lo
    dgrad[...] = dot3(hth[...], dh[...], dl[...], NN)
    o2 = local(dgrad, gd_o, 5)
    outs = [o2]
    for i, (c, o) in enumerate(((p_g, gg_o), (p_u, gu_o))):
        c.wait_recv()
        hi, lo = split(far[i])
        bh[i, pl.ds(ROWS, ROWS), :] = hi
        bl[i, pl.ds(ROWS, ROWS), :] = lo
        wgrad[i] = dot3(xth[...], bh[i], bl[i], NN)[:, :H]
        outs.append(local(wgrad.at[i], o, 6 + i))

    for i, (c, src, dst, o) in enumerate(((g0, op, o_own, out_o), (g1, gp, g_own, gtok_o))):
        for d in c:
            d.wait_recv()
        total = src[pl.ds(hrow, 16), :]
        for k in range(7):
            total = total + rg[i, k]
        dst[...] = total
        outs.append(local(dst, o, 8 + i))
    for c in outs:
        c.wait()
    for c in sent:
        c.wait_send()


def shards(tokens, cotangent, w_gate, w_up, w_down):
    v = pltpu.VMEM
    dma = pltpu.SemaphoreType.DMA
    scratch = [
        v((ROWS, W), F32), v((ROWS, W), F32), v((2 * ROWS, W), BF16), v((2 * ROWS, W), BF16),
        v((W, H), F32), v((W, H), F32), v((H, W), F32),
        v((W, HP), BF16), v((W, HP), BF16), v((W, HP), BF16), v((W, HP), BF16),
        v((HP, W), BF16), v((HP, W), BF16),
        v((3, ROWS, HP), F32), v((3, 32, HP), F32), v((3, 3, 8, HP), F32), v((3, 3, 16, HP), F32),
        v((3, 8, HP), F32), v((3, 32, HP), F32), v((3, 16, HP), F32), v((8, 128), F32), v((3, ROWS, HP), F32),
        v((W, ROWS), F32), v((320, ROWS), F32), v((ROWS, W), F32), v((HP, ROWS), F32), v((432, ROWS), F32),
        v((2, ROWS, HP), F32),
        v((640, 256), BF16), v((8, 128), BF16), v((864, 256), BF16), v((8, 128), BF16),
        v((2, 256, HP), BF16), v((2, 256, HP), BF16), v((256, W), BF16), v((256, W), BF16),
        v((ROWS, W), F32), v((ROWS, W), F32), v((2, 7, 16, W), F32), v((16, W), F32), v((16, W), F32),
        v((2, 320, H), F32), v((432, W), F32),
        dma((14,)), dma((14,)), dma((3, 8)), dma((3, 8)), dma((3, 8)), dma((3, 8)),
        dma((2, 7)), dma((2, 7)), dma((5,)), dma((5,)), dma((10,)),
    ]
    any_ = pl.BlockSpec(memory_space=pl.ANY)
    out, gtok, gg, gu, gd = pl.pallas_call(
        kernel,
        out_shape=[
            jax.ShapeDtypeStruct((16, W), F32), jax.ShapeDtypeStruct((16, W), F32),
            jax.ShapeDtypeStruct((320, H), F32), jax.ShapeDtypeStruct((320, H), F32),
            jax.ShapeDtypeStruct((432, W), F32),
        ],
        in_specs=[any_] * 5,
        out_specs=[any_] * 5,
        scratch_shapes=scratch,
        compiler_params=pltpu.CompilerParams(
            collective_id=0, has_side_effects=True, vmem_limit_bytes=56 << 20
        ),
    )(tokens, cotangent, w_gate, w_up, w_down)
    return out, gtok, gg[None, None], gu[None, None], gd[None, None]


def solution(mesh):
    return jax.shard_map(
        shards,
        mesh=mesh,
        in_specs=(
            P(("rep", "hid"), "width"), P(("rep", "hid"), "width"),
            P("width", "hid"), P("width", "hid"), P("hid", "width"),
        ),
        out_specs=(
            P(("rep", "hid"), "width"), P(("rep", "hid"), "width"),
            P("width", "rep", None, "hid"), P("width", "rep", None, "hid"),
            P("hid", "rep", None, "width"),
        ),
        check_vma=False,
    )
```

```python
import functools

import jax
import jax.numpy as jnp
from jax import lax
from jax.experimental import pallas as pl
from jax.experimental.pallas import tpu as pltpu
from jax.sharding import PartitionSpec as P

MESH = pl.DeviceIdType.MESH
F32 = jnp.float32
BF16 = jnp.bfloat16
NN = (((1,), (0,)), ((), ()))
NT = (((1,), (1,)), ((), ()))
ROWS = 128
W = 640
H = 864
HP = 896
X_OFFS = [(a, b) for a in range(4) for b in range(2) if (a, b) != (0, 0)]


def split(v):
    hi = v.astype(BF16)
    return hi, (v - hi.astype(F32)).astype(BF16)


def dot(a, b, dims):
    return lax.dot_general(a, b, dims, preferred_element_type=F32)


def dot3(stack, b_hi, b_lo, dims):
    m = stack.shape[0] // 2
    both = dot(stack, b_hi, dims)
    return both[:m] + both[m:] + dot(stack[:m], b_lo, dims)


def kernel(
    tok_in, cot_in, wg_in, wu_in, wd_in,
    out_o, gtok_o, gg_o, gu_o, gd_o,
    xf, df, xs, ds_, wgf, wuf, wdf, wgh, wgl, wuh, wul, wdh, wdl,
    part, r1, r2, r3, r4, s1, s3, full,
    xt, xt_far, dy_far, ht, ht_far, far,
    xth, hth, bh, bl, dh, dl,
    op, gp, rg,
    a_s, a_r, c_s, c_r, e_s, e_r, g_s, g_r, p_s, p_r, l_s,
):
    rep = lax.axis_index("rep")
    w = lax.axis_index("width")
    h = lax.axis_index("hid")
    y, xl = w // 2, w % 2
    z, xh = h // 2, h % 2

    def ydev(k):
        return (rep, ((y + k) % 4) * 2 + xl, h)

    xdev = (rep, y * 2 + (1 - xl), h)

    def hdev(off):
        return (rep, w, ((z + off[0]) % 4) * 2 + (xh + off[1]) % 2)

    pdev = (1 - rep, w, h)
    sent = []

    def send(src, dst, s, r, device):
        c = pltpu.make_async_remote_copy(
            src_ref=src, dst_ref=dst, send_sem=s, recv_sem=r,
            device_id=device, device_id_type=MESH,
        )
        c.start()
        sent.append(c)
        return c

    def local(src, dst, i):
        c = pltpu.make_async_copy(src, dst, l_s.at[i])
        c.start()
        return c

    hrow = pl.multiple_of(h * 16, 16)
    lx = local(tok_in, xf.at[pl.ds(hrow, 16)], 0)
    ly = local(cot_in, df.at[pl.ds(hrow, 16)], 1)
    lg = local(wg_in, wgf, 2)
    lu = local(wu_in, wuf, 3)
    ld = local(wd_in, wdf, 4)

    barrier = pltpu.get_barrier_semaphore()
    peers = [ydev(k) for k in (1, 2, 3)] + [xdev] + [hdev(o) for o in X_OFFS] + [pdev]
    for d in peers:
        pl.semaphore_signal(barrier, inc=1, device_id=d, device_id_type=MESH)
    pl.semaphore_wait(barrier, len(peers))

    ax = [send(tok_in, xf.at[pl.ds(hrow, 16)], a_s.at[k], a_r.at[k], hdev(o)) for k, o in enumerate(X_OFFS)]
    ad = [send(cot_in, df.at[pl.ds(hrow, 16)], a_s.at[7 + k], a_r.at[7 + k], hdev(o)) for k, o in enumerate(X_OFFS)]

    def halves(src, hi_ref, lo_ref):
        step = 32

        def body(i, _):
            at = pl.multiple_of(i * step, step)
            hi, lo = split(src[pl.ds(at, step), :])
            hi_ref[pl.ds(at, step), :] = hi
            lo_ref[pl.ds(at, step), :] = lo
            return 0

        lax.fori_loop(0, H // step, body, 0)

    for ref in (wgh, wgl, wuh, wul, wdh, wdl):
        ref[pl.ds(H, HP - H), :] = jnp.zeros((HP - H, W), BF16)
    lg.wait()
    halves(wgf, wgh, wgl)
    lu.wait()
    halves(wuf, wuh, wul)

    def scatter(a):
        c = [
            send(
                part.at[a, pl.ds(pl.multiple_of(32 * (1 - xl), 32), 32)], r1.at[a],
                c_s.at[a, 0], c_r.at[a, 0], xdev,
            )
        ]
        for k in (1, 2, 3):
            row = pl.multiple_of(64 + 16 * ((y + k) % 4), 16)
            c.append(
                send(part.at[a, pl.ds(row, 16)], r3.at[a, k - 1], c_s.at[a, k], c_r.at[a, k], ydev(k))
            )
        return c

    lx.wait()
    for c in ax:
        c.wait_recv()
    hi, lo = split(xf[...])
    xs[pl.ds(0, ROWS), :] = hi
    xs[pl.ds(ROWS, ROWS), :] = lo
    part[0] = dot3(xs[...], wgh[...], wgl[...], NT)
    c0 = scatter(0)
    part[1] = dot3(xs[...], wuh[...], wul[...], NT)
    c1 = scatter(1)
    ld.wait()
    halves(wdf, wdh, wdl)
    ly.wait()
    for c in ad:
        c.wait_recv()
    hi, lo = split(df[...])
    ds_[pl.ds(0, ROWS), :] = hi
    ds_[pl.ds(ROWS, ROWS), :] = lo
    part[2] = dot3(ds_[...], wdh[...], wdl[...], NT)
    c2 = scatter(2)
    p_dy = send(df, dy_far, p_s.at[0], p_r.at[0], pdev)

    def second(a, first):
        first[0].wait_recv()
        s1[a] = part[a, pl.ds(pl.multiple_of(32 * xl, 32), 32), :] + r1[a]
        c = []
        for k in (1, 2, 3):
            row = pl.multiple_of(8 * ((y + k) % 4), 8)
            c.append(
                send(s1.at[a, pl.ds(row, 8)], r2.at[a, k - 1], c_s.at[a, 3 + k], c_r.at[a, 3 + k], ydev(k))
            )
        for d in first[1:]:
            d.wait_recv()
        s3[a] = part[a, pl.ds(pl.multiple_of(64 + 16 * y, 16), 16), :] + r3[a, 0] + r3[a, 1] + r3[a, 2]
        c.append(
            send(
                s3.at[a, pl.ds(pl.multiple_of(8 * (1 - xl), 8), 8)], r4.at[a],
                c_s.at[a, 7], c_r.at[a, 7], xdev,
            )
        )
        return c

    def summed(a, c):
        for d in c:
            d.wait_recv()
        top = s1[a, pl.ds(pl.multiple_of(8 * y, 8), 8), :] + r2[a, 0] + r2[a, 1] + r2[a, 2]
        low = s3[a, pl.ds(pl.multiple_of(8 * xl, 8), 8), :] + r4[a]
        return jnp.concatenate([top, low], axis=0)

    top_row = pl.multiple_of(8 * (4 * xl + y), 8)
    low_row = pl.multiple_of(64 + 8 * (2 * y + xl), 8)
    low_pair = pl.multiple_of(64 + 16 * y, 16)
    top_half = pl.multiple_of(32 * xl, 32)

    def gather(a, value):
        full[a, pl.ds(top_row, 8), :] = value[:8]
        full[a, pl.ds(low_row, 8), :] = value[8:]
        c = [
            send(full.at[a, pl.ds(low_row, 8)], full.at[a, pl.ds(low_row, 8)], e_s.at[a, 0], e_r.at[a, 0], xdev)
        ]
        for k in (1, 2, 3):
            c.append(
                send(full.at[a, pl.ds(top_row, 8)], full.at[a, pl.ds(top_row, 8)], e_s.at[a, k], e_r.at[a, k], ydev(k))
            )
        return c

    def gather_on(a, first):
        first[0].wait_recv()
        c = []
        for k in (1, 2, 3):
            c.append(
                send(
                    full.at[a, pl.ds(low_pair, 16)], full.at[a, pl.ds(low_pair, 16)],
                    e_s.at[a, 3 + k], e_r.at[a, 3 + k], ydev(k),
                )
            )
        for d in first[1:]:
            d.wait_recv()
        c.append(
            send(
                full.at[a, pl.ds(top_half, 32)], full.at[a, pl.ds(top_half, 32)],
                e_s.at[a, 7], e_r.at[a, 7], xdev,
            )
        )
        return c

    d0 = second(0, c0)
    d1 = second(1, c1)
    d2 = second(2, c2)
    for j in range(5):
        xt[pl.ds(128 * j, 128), :] = xf[:, pl.ds(128 * j, 128)].T
    half_x = pl.multiple_of(320 * rep, 64)
    far_x = pl.multiple_of(320 * (1 - rep), 64)
    p_x = send(xt.at[pl.ds(far_x, 320)], xt_far, p_s.at[1], p_r.at[1], pdev)

    gate = summed(0, d0)
    up = summed(1, d1)
    logistic = 1.0 / (1.0 + jnp.exp(-gate))
    e0 = gather(0, gate * logistic * up)
    back = summed(2, d2)
    e1 = gather(1, back * up * logistic * (1.0 + gate * (1.0 - logistic)))
    e2 = gather(2, back * gate * logistic)

    f0 = gather_on(0, e0)
    f1 = gather_on(1, e1)
    f2 = gather_on(2, e2)

    def reduce_rows(src, i):
        c = []
        for k, o in enumerate(X_OFFS):
            row = pl.multiple_of(16 * (((z + o[0]) % 4) * 2 + (xh + o[1]) % 2), 16)
            c.append(send(src.at[pl.ds(row, 16)], rg.at[i, k], g_s.at[i, k], g_r.at[i, k], hdev(o)))
        return c

    for d in f0:
        d.wait_recv()
    hid = full[0]
    hi, lo = split(hid)
    op[...] = dot3(jnp.concatenate([hi, lo], axis=0), wdh[...], wdl[...], NN)
    g0 = reduce_rows(op, 0)
    for j in range(7):
        ht[pl.ds(128 * j, 128), :] = full[0, :, pl.ds(128 * j, 128)].T
    half_h = pl.multiple_of(432 * rep, 16)
    far_h = pl.multiple_of(432 * (1 - rep), 16)
    p_h = send(ht.at[pl.ds(far_h, 432)], ht_far, p_s.at[2], p_r.at[2], pdev)

    for d in f1:
        d.wait_recv()
    p_g = send(full.at[1], far.at[0], p_s.at[3], p_r.at[3], pdev)
    hi, lo = split(full[1])
    bh[0, pl.ds(0, ROWS), :] = hi
    bl[0, pl.ds(0, ROWS), :] = lo
    acc = dot3(jnp.concatenate([hi, lo], axis=0), wgh[...], wgl[...], NN)
    for d in f2:
        d.wait_recv()
    p_u = send(full.at[2], far.at[1], p_s.at[4], p_r.at[4], pdev)
    hi, lo = split(full[2])
    bh[1, pl.ds(0, ROWS), :] = hi
    bl[1, pl.ds(0, ROWS), :] = lo
    gp[...] = acc + dot3(jnp.concatenate([hi, lo], axis=0), wuh[...], wul[...], NN)
    g1 = reduce_rows(gp, 1)

    p_x.wait_recv()
    for ref, at in ((xt.at[pl.ds(half_x, 320)], 0), (xt_far, 128)):
        hi, lo = split(ref[...])
        xth[pl.ds(0, 320), pl.ds(at, 128)] = hi
        xth[pl.ds(320, 320), pl.ds(at, 128)] = lo
    p_dy.wait_recv()
    dh[pl.ds(0, ROWS), :] = ds_[pl.ds(0, ROWS), :]
    dl[pl.ds(0, ROWS), :] = ds_[pl.ds(ROWS, ROWS), :]
    hi, lo = split(dy_far[...])
    dh[pl.ds(ROWS, ROWS), :] = hi
    dl[pl.ds(ROWS, ROWS), :] = lo
    p_h.wait_recv()
    for ref, at in ((ht.at[pl.ds(half_h, 432)], 0), (ht_far, 128)):
        hi, lo = split(ref[...])
        hth[pl.ds(0, 432), pl.ds(at, 128)] = hi
        hth[pl.ds(432, 432), pl.ds(at, 128)] = lo
    gd_o[...] = dot3(hth[...], dh[...], dl[...], NN)
    for i, (c, o) in enumerate(((p_g, gg_o), (p_u, gu_o))):
        c.wait_recv()
        hi, lo = split(far[i])
        bh[i, pl.ds(ROWS, ROWS), :] = hi
        bl[i, pl.ds(ROWS, ROWS), :] = lo
        o[...] = dot3(xth[...], bh[i], bl[i], NN)[:, :H]

    for i, (c, src, o) in enumerate(((g0, op, out_o), (g1, gp, gtok_o))):
        for d in c:
            d.wait_recv()
        total = src[pl.ds(hrow, 16), :]
        for k in range(7):
            total = total + rg[i, k]
        o[...] = total
    for c in sent:
        c.wait_send()


def write(*refs):
    copies = [pltpu.make_async_copy(refs[i], refs[5 + i], refs[10].at[i]) for i in range(5)]
    for c in copies:
        c.start()
    for c in copies:
        c.wait()


def shards(tokens, cotangent, w_gate, w_up, w_down):
    v = pltpu.VMEM
    dma = pltpu.SemaphoreType.DMA
    scratch = [
        v((ROWS, W), F32), v((ROWS, W), F32), v((2 * ROWS, W), BF16), v((2 * ROWS, W), BF16),
        *[v((H, W), F32)] * 3, *[v((HP, W), BF16)] * 6,
        v((3, ROWS, HP), F32), v((3, 32, HP), F32), v((3, 3, 8, HP), F32), v((3, 3, 16, HP), F32),
        v((3, 8, HP), F32), v((3, 32, HP), F32), v((3, 16, HP), F32), v((3, ROWS, HP), F32),
        v((W, ROWS), F32), v((320, ROWS), F32), v((ROWS, W), F32), v((HP, ROWS), F32), v((432, ROWS), F32),
        v((2, ROWS, HP), F32),
        v((640, 256), BF16), v((864, 256), BF16),
        v((2, 256, HP), BF16), v((2, 256, HP), BF16), v((256, W), BF16), v((256, W), BF16),
        v((ROWS, W), F32), v((ROWS, W), F32), v((2, 7, 16, W), F32),
        dma((14,)), dma((14,)), dma((3, 8)), dma((3, 8)), dma((3, 8)), dma((3, 8)),
        dma((2, 7)), dma((2, 7)), dma((5,)), dma((5,)), dma((5,)),
    ]
    any_ = pl.BlockSpec(memory_space=pl.ANY)
    vmem = pl.BlockSpec(memory_space=pltpu.VMEM)
    hbm = pl.BlockSpec(memory_space=pltpu.HBM)
    shapes = [(16, W), (16, W), (320, H), (320, H), (432, W)]
    results = pl.pallas_call(
        kernel,
        out_shape=[v(s, F32) for s in shapes],
        in_specs=[hbm] * 5,
        out_specs=[vmem] * 5,
        scratch_shapes=scratch,
        compiler_params=pltpu.CompilerParams(
            collective_id=0, has_side_effects=True, vmem_limit_bytes=48 << 20
        ),
    )(*[pltpu.with_memory_space_constraint(a, pltpu.HBM) for a in (tokens, cotangent, w_gate.T, w_up.T, w_down)])
    results = [pltpu.with_memory_space_constraint(r, pltpu.VMEM) for r in results]
    out, gtok, gg, gu, gd = pl.pallas_call(
        write,
        out_shape=[jax.ShapeDtypeStruct(s, F32) for s in shapes],
        in_specs=[vmem] * 5,
        out_specs=[any_] * 5,
        scratch_shapes=[dma((5,))],
    )(*results)
    return out, gtok, gg[None, None], gu[None, None], gd[None, None]


def solution(mesh):
    return jax.shard_map(
        shards,
        mesh=mesh,
        in_specs=(
            P(("rep", "hid"), "width"), P(("rep", "hid"), "width"),
            P("width", "hid"), P("width", "hid"), P("hid", "width"),
        ),
        out_specs=(
            P(("rep", "hid"), "width"), P(("rep", "hid"), "width"),
            P("width", "rep", None, "hid"), P("width", "rep", None, "hid"),
            P("hid", "rep", None, "width"),
        ),
        check_vma=False,
    )
```

```python
import functools

import jax
import jax.numpy as jnp
from jax import lax
from jax.experimental import pallas as pl
from jax.experimental.pallas import tpu as pltpu
from jax.sharding import PartitionSpec as P

MESH = pl.DeviceIdType.MESH
F32 = jnp.float32
BF16 = jnp.bfloat16
NN = (((1,), (0,)), ((), ()))
NT = (((1,), (1,)), ((), ()))
ROWS = 128
W = 640
H = 864
HP = 896
C = 64
CX = 384
LX, LY = pl.ds(0, CX), pl.ds(CX, HP - CX)
GROUPS = ((0, 2), (2, 1))
GROUPS_BACK = ((0, 1), (1, 2))
H_OFFS = [(a, b) for a in range(4) for b in range(2) if (a, b) != (0, 0)]


def split(v):
    hi = v.astype(BF16)
    return hi, (v - hi.astype(F32)).astype(BF16)


def dot(a, b, dims):
    return lax.dot_general(a, b, dims, preferred_element_type=F32)


def dot3(stack, b_hi, b_lo, dims):
    m = stack.shape[0] // 2
    both = dot(stack, b_hi, dims)
    return both[:m] + both[m:] + dot(stack[:m], b_lo, dims)


def kernel(
    tok_in, cot_in, wg_in, wu_in, wd_in,
    out_o, gtok_o, gg_o, gu_o, gd_o,
    xf, df, xs, ds_, wgf, wuf, wdf, wgh, wgl, wuh, wul, wdh, wdl,
    part, r1, r2, r3, r4, s1, s3, full,
    xt, xt_far, dy_far, ht, ht_far, far,
    xth, hth, bh, bl, dh, dl,
    op, rg,
    a_s, a_r, c_s, c_r, e_s, e_r, g_s, g_r, p_s, p_r, l_s,
):
    rep = lax.axis_index("rep")
    w = lax.axis_index("width")
    h = lax.axis_index("hid")
    y, xl = w // 2, w % 2
    z, xh = h // 2, h % 2

    def ydev(k):
        return (rep, ((y + k) % 4) * 2 + xl, h)

    xdev = (rep, y * 2 + (1 - xl), h)

    def hindex(off):
        return ((z + off[0]) % 4) * 2 + (xh + off[1]) % 2

    def hdev(off):
        return (rep, w, hindex(off))

    pdev = (1 - rep, w, h)
    sent = []

    def send(src, dst, s, r, device):
        c = pltpu.make_async_remote_copy(
            src_ref=src, dst_ref=dst, send_sem=s, recv_sem=r,
            device_id=device, device_id_type=MESH,
        )
        c.start()
        sent.append(c)
        return c

    def local(src, dst, i):
        c = pltpu.make_async_copy(src, dst, l_s.at[i])
        c.start()
        return c

    def row8(k):
        return pl.ds(pl.multiple_of(8 * k, 8), 8)

    def arrived(copies):
        for d in copies:
            d.wait_recv()

    def rows_of(c):
        return pl.ds(pl.multiple_of(C * c + 8 * h, 8), 8)

    lx = [local(tok_in.at[pl.ds(8 * c, 8)], xf.at[rows_of(c)], c) for c in range(2)]
    ly = [local(cot_in.at[pl.ds(8 * c, 8)], df.at[rows_of(c)], 2 + c) for c in range(2)]
    lg = local(wg_in, wgf, 4)
    lu = local(wu_in, wuf, 5)
    ld = local(wd_in, wdf, 6)

    barrier = pltpu.get_barrier_semaphore()
    peers = [ydev(k) for k in (1, 2, 3)] + [xdev] + [hdev(o) for o in H_OFFS] + [pdev]
    for d in peers:
        pl.semaphore_signal(barrier, inc=1, device_id=d, device_id_type=MESH)
    pl.semaphore_wait(barrier, len(peers))

    def spread(src, dst, c, i):
        return [
            send(src.at[pl.ds(8 * c, 8)], dst.at[rows_of(c)], a_s.at[i, k], a_r.at[i, k], hdev(o))
            for k, o in enumerate(H_OFFS)
        ]

    ax, ad = [], []
    for c in range(2):
        ax.append(spread(tok_in, xf, c, 2 * c))
        ad.append(spread(cot_in, df, c, 2 * c + 1))

    def halves(src, hi_ref, lo_ref):
        step = 32

        def body(i, _):
            at = pl.multiple_of(i * step, step)
            hi, lo = split(src[pl.ds(at, step), :])
            hi_ref[pl.ds(at, step), :] = hi
            lo_ref[pl.ds(at, step), :] = lo
            return 0

        lax.fori_loop(0, H // step, body, 0)

    def stacked(src, dst, c):
        hi, lo = split(src[pl.ds(C * c, C), :])
        dst[c, pl.ds(0, C), :] = hi
        dst[c, pl.ds(C, C), :] = lo

    def halved(v):
        return v.reshape(2, C // 2, v.shape[1])

    def scatter(c, g):
        lo, n = GROUPS[g]
        arrays = pl.ds(lo, n)
        out = [
            send(
                part.at[c, arrays, 1 - xl, :, LX], r1.at[c, arrays],
                c_s.at[c, g, 0], c_r.at[c, g, 0], xdev,
            )
        ]
        for k in (1, 2, 3):
            out.append(
                send(
                    part.at[c, arrays, :, row8((y + k) % 4), LY], r3.at[c, k - 1, arrays],
                    c_s.at[c, g, k], c_r.at[c, g, k], ydev(k),
                )
            )
        return out

    def scatter_on(c, g, first):
        lo, n = GROUPS[g]
        arrays = pl.ds(lo, n)
        arrived(first[:1])
        for a in range(lo, lo + n):
            s1[c, a] = part[c, a, xl, :, LX] + r1[c, a]
        out = []
        for k in (1, 2, 3):
            out.append(
                send(
                    s1.at[c, arrays, row8((y + k) % 4)], r2.at[c, k - 1, arrays],
                    c_s.at[c, g, 3 + k], c_r.at[c, g, 3 + k], ydev(k),
                )
            )
        arrived(first[1:])
        for a in range(lo, lo + n):
            s3[c, a] = part[c, a, :, row8(y), LY] + r3[c, 0, a] + r3[c, 1, a] + r3[c, 2, a]
        out.append(
            send(
                s3.at[c, arrays, 1 - xl], r4.at[c, arrays],
                c_s.at[c, g, 7], c_r.at[c, g, 7], xdev,
            )
        )
        return out

    def summed(c, a):
        left = s1[c, a, row8(y), :] + r2[c, 0, a] + r2[c, 1, a] + r2[c, 2, a]
        right = s3[c, a, xl] + r4[c, a]
        return jnp.concatenate([left, right], axis=1)

    def gather(c, g):
        lo, n = GROUPS_BACK[g]
        arrays = pl.ds(lo, n)
        mine = full.at[c, arrays, xl, row8(y), LY]
        out = [send(mine, mine, e_s.at[c, g, 0], e_r.at[c, g, 0], xdev)]
        mine = full.at[c, arrays, xl, row8(y), LX]
        for k in (1, 2, 3):
            out.append(send(mine, mine, e_s.at[c, g, k], e_r.at[c, g, k], ydev(k)))
        return out

    def gather_on(c, g, first):
        lo, n = GROUPS_BACK[g]
        arrays = pl.ds(lo, n)
        out = []
        arrived(first[:1])
        pair = full.at[c, arrays, :, row8(y), LY]
        for k in (1, 2, 3):
            out.append(send(pair, pair, e_s.at[c, g, 3 + k], e_r.at[c, g, 3 + k], ydev(k)))
        arrived(first[1:])
        half = full.at[c, arrays, xl, :, LX]
        out.append(send(half, half, e_s.at[c, g, 7], e_r.at[c, g, 7], xdev))
        return out

    def activate(c):
        gate = summed(c, 0)
        up = summed(c, 1)
        logistic = 1.0 / (1.0 + jnp.exp(-gate))
        full[c, 0, xl, row8(y), :] = gate * logistic * up
        return gather(c, 0), (gate, up, logistic)

    def derive(c, saved):
        gate, up, logistic = saved
        back = summed(c, 2)
        full[c, 1, xl, row8(y), :] = back * up * logistic * (1.0 + gate * (1.0 - logistic))
        full[c, 2, xl, row8(y), :] = back * gate * logistic
        return gather(c, 1)

    def whole(c, a):
        return full[c, a].reshape(C, HP)

    def reduce_rows(i, c):
        return [
            send(
                op.at[i, c, row8(hindex(o))], rg.at[i, c, k],
                g_s.at[i, c, k], g_r.at[i, c, k], hdev(o),
            )
            for k, o in enumerate(H_OFFS)
        ]

    def project(c):
        hi, lo = split(whole(c, 0))
        op[0, c] = dot3(jnp.concatenate([hi, lo], axis=0), wdh[...], wdl[...], NN)
        return reduce_rows(0, c)

    def pull_back(c):
        acc = None
        for i, (wh, wl) in enumerate(((wgh, wgl), (wuh, wul))):
            hi, lo = split(whole(c, 1 + i))
            bh[i, pl.ds(C * c, C), :] = hi
            bl[i, pl.ds(C * c, C), :] = lo
            term = dot3(jnp.concatenate([hi, lo], axis=0), wh[...], wl[...], NN)
            acc = term if acc is None else acc + term
        op[1, c] = acc
        return reduce_rows(1, c)

    def gate_up(c):
        lx[c].wait()
        arrived(ax[c])
        stacked(xf, xs, c)
        part[c, 0] = halved(dot3(xs[c], wgh[...], wgl[...], NT))
        part[c, 1] = halved(dot3(xs[c], wuh[...], wul[...], NT))
        return scatter(c, 0)

    def back_part(c):
        ly[c].wait()
        arrived(ad[c])
        stacked(df, ds_, c)
        part[c, 2] = halved(dot3(ds_[c], wdh[...], wdl[...], NT))
        return scatter(c, 1)

    for ref in (wgh, wgl, wuh, wul, wdh, wdl):
        ref[pl.ds(H, HP - H), :] = jnp.zeros((HP - H, W), BF16)
    lg.wait()
    halves(wgf, wgh, wgl)
    lu.wait()
    halves(wuf, wuh, wul)
    c00 = gate_up(0)
    ld.wait()
    halves(wdf, wdh, wdl)
    c01 = back_part(0)
    c10 = gate_up(1)
    d00 = scatter_on(0, 0, c00)
    c11 = back_part(1)
    d01 = scatter_on(0, 1, c01)
    p_dy = send(df, dy_far, p_s.at[0], p_r.at[0], pdev)
    arrived(d00)
    e00, saved0 = activate(0)
    d10 = scatter_on(1, 0, c10)
    arrived(d01)
    e01 = derive(0, saved0)
    f00 = gather_on(0, 0, e00)
    d11 = scatter_on(1, 1, c11)
    arrived(d10)
    e10, saved1 = activate(1)
    f01 = gather_on(0, 1, e01)
    arrived(d11)
    e11 = derive(1, saved1)
    for j in range(5):
        xt[pl.ds(128 * j, 128), :] = xf[:, pl.ds(128 * j, 128)].T
    half_x = pl.multiple_of(320 * rep, 64)
    far_x = pl.multiple_of(320 * (1 - rep), 64)
    p_x = send(xt.at[pl.ds(far_x, 320)], xt_far, p_s.at[1], p_r.at[1], pdev)
    f10 = gather_on(1, 0, e10)
    arrived(f00)
    g00 = project(0)
    f11 = gather_on(1, 1, e11)
    arrived(f01)
    g10 = pull_back(0)
    arrived(f10)
    g01 = project(1)
    for j in range(7):
        lanes = pl.ds(128 * j, 128)
        block = jnp.concatenate([full[0, 0, :, :, lanes].reshape(C, 128), full[1, 0, :, :, lanes].reshape(C, 128)], axis=0)
        ht[pl.ds(128 * j, 128), :] = block.T
    half_h = pl.multiple_of(432 * rep, 16)
    far_h = pl.multiple_of(432 * (1 - rep), 16)
    p_h = send(ht.at[pl.ds(far_h, 432)], ht_far, p_s.at[2], p_r.at[2], pdev)
    arrived(f11)
    p_gu = send(full.at[:, pl.ds(1, 2)], far, p_s.at[3], p_r.at[3], pdev)
    g11 = pull_back(1)

    p_x.wait_recv()
    for ref, at in ((xt.at[pl.ds(half_x, 320)], 0), (xt_far, ROWS)):
        hi, lo = split(ref[...])
        xth[pl.ds(0, 320), pl.ds(at, ROWS)] = hi
        xth[pl.ds(320, 320), pl.ds(at, ROWS)] = lo
    p_dy.wait_recv()
    for c in range(2):
        dh[pl.ds(C * c, C), :] = ds_[c, pl.ds(0, C), :]
        dl[pl.ds(C * c, C), :] = ds_[c, pl.ds(C, C), :]
    hi, lo = split(dy_far[...])
    dh[pl.ds(ROWS, ROWS), :] = hi
    dl[pl.ds(ROWS, ROWS), :] = lo
    p_h.wait_recv()
    for ref, at in ((ht.at[pl.ds(half_h, 432)], 0), (ht_far, ROWS)):
        hi, lo = split(ref[...])
        hth[pl.ds(0, 432), pl.ds(at, ROWS)] = hi
        hth[pl.ds(432, 432), pl.ds(at, ROWS)] = lo
    gd_o[...] = dot3(hth[...], dh[...], dl[...], NN)
    p_gu.wait_recv()
    for i, o in enumerate((gg_o, gu_o)):
        for c in range(2):
            hi, lo = split(far[c, i].reshape(C, HP))
            bh[i, pl.ds(ROWS + C * c, C), :] = hi
            bl[i, pl.ds(ROWS + C * c, C), :] = lo
        o[...] = dot3(xth[...], bh[i], bl[i], NN)[:, :H]

    for i, c, copies, o in ((0, 0, g00, out_o), (1, 0, g10, gtok_o), (0, 1, g01, out_o), (1, 1, g11, gtok_o)):
        arrived(copies)
        total = op[i, c, row8(h), :]
        for k in range(7):
            total = total + rg[i, c, k]
        o[pl.ds(8 * c, 8), :] = total
    for c in sent:
        c.wait_send()


def write(*refs):
    copies = [pltpu.make_async_copy(refs[i], refs[5 + i], refs[10].at[i]) for i in range(5)]
    for c in copies:
        c.start()
    for c in copies:
        c.wait()


def shards(tokens, cotangent, w_gate, w_up, w_down):
    v = pltpu.VMEM
    dma = pltpu.SemaphoreType.DMA
    cy = HP - CX
    scratch = [
        v((ROWS, W), F32), v((ROWS, W), F32), v((2, 2 * C, W), BF16), v((2, 2 * C, W), BF16),
        *[v((H, W), F32)] * 3, *[v((HP, W), BF16)] * 6,
        v((2, 3, 2, 32, HP), F32), v((2, 3, 32, CX), F32), v((2, 3, 3, 8, CX), F32),
        v((2, 3, 3, 2, 8, cy), F32), v((2, 3, 8, cy), F32), v((2, 3, 32, CX), F32),
        v((2, 3, 2, 8, cy), F32), v((2, 3, 2, 32, HP), F32),
        v((W, ROWS), F32), v((320, ROWS), F32), v((ROWS, W), F32), v((HP, ROWS), F32), v((432, ROWS), F32),
        v((2, 2, 2, 32, HP), F32),
        v((640, 256), BF16), v((864, 256), BF16),
        v((2, 256, HP), BF16), v((2, 256, HP), BF16), v((256, W), BF16), v((256, W), BF16),
        v((2, 2, C, W), F32), v((2, 2, 7, 8, W), F32),
        dma((4, 7)), dma((4, 7)), dma((2, 2, 8)), dma((2, 2, 8)), dma((2, 2, 8)), dma((2, 2, 8)),
        dma((2, 2, 7)), dma((2, 2, 7)), dma((4,)), dma((4,)), dma((7,)),
    ]
    any_ = pl.BlockSpec(memory_space=pl.ANY)
    vmem = pl.BlockSpec(memory_space=pltpu.VMEM)
    hbm = pl.BlockSpec(memory_space=pltpu.HBM)
    shapes = [(16, W), (16, W), (320, H), (320, H), (432, W)]
    results = pl.pallas_call(
        kernel,
        out_shape=[v(s, F32) for s in shapes],
        in_specs=[hbm] * 5,
        out_specs=[vmem] * 5,
        scratch_shapes=scratch,
        compiler_params=pltpu.CompilerParams(
            collective_id=0, has_side_effects=True, vmem_limit_bytes=48 << 20
        ),
    )(*[pltpu.with_memory_space_constraint(a, pltpu.HBM) for a in (tokens, cotangent, w_gate.T, w_up.T, w_down)])
    results = [pltpu.with_memory_space_constraint(r, pltpu.VMEM) for r in results]
    out, gtok, gg, gu, gd = pl.pallas_call(
        write,
        out_shape=[jax.ShapeDtypeStruct(s, F32) for s in shapes],
        in_specs=[vmem] * 5,
        out_specs=[any_] * 5,
        scratch_shapes=[dma((5,))],
    )(*results)
    return out, gtok, gg[None, None], gu[None, None], gd[None, None]


def solution(mesh):
    return jax.shard_map(
        shards,
        mesh=mesh,
        in_specs=(
            P(("rep", "hid"), "width"), P(("rep", "hid"), "width"),
            P("width", "hid"), P("width", "hid"), P("hid", "width"),
        ),
        out_specs=(
            P(("rep", "hid"), "width"), P(("rep", "hid"), "width"),
            P("width", "rep", None, "hid"), P("width", "rep", None, "hid"),
            P("hid", "rep", None, "width"),
        ),
        check_vma=False,
    )
```

```python
import functools

import jax
import jax.numpy as jnp
from jax import lax
from jax.experimental import pallas as pl
from jax.experimental.pallas import tpu as pltpu
from jax.sharding import PartitionSpec as P

MESH = pl.DeviceIdType.MESH
F32 = jnp.float32
BF16 = jnp.bfloat16
NN = (((1,), (0,)), ((), ()))
NT = (((1,), (1,)), ((), ()))
ROWS = 128
W = 640
H = 864
HP = 896
C = 64
CX = 512
EX = 384
SX, SY = pl.ds(0, CX), pl.ds(CX, HP - CX)
GX, GY = pl.ds(0, EX), pl.ds(EX, HP - EX)
GROUPS = ((0, 2), (2, 1))
GROUPS_BACK = ((0, 1), (1, 2))
PIECES = (1, 1, 1, 1, 1)
ORDER = ("fx", "gu0", "fd", "bk0", "gu1", "bk1", "s00", "s01", "s10", "s11", "act0", "dy", "der0", "act1", "der1", "f00", "f10", "f11", "f01", "pr0", "xt", "pr1", "pb1", "r01", "pb0", "r11", "ht")


def split(v):
    hi = v.astype(BF16)
    return hi, (v - hi.astype(F32)).astype(BF16)


def dot(a, b, dims):
    return lax.dot_general(a, b, dims, preferred_element_type=F32)


def dot3(stack, b_hi, b_lo, dims):
    m = stack.shape[0] // 2
    both = dot(stack, b_hi, dims)
    return both[:m] + both[m:] + dot(stack[:m], b_lo, dims)


def kernel(
    tok_in, cot_in, wg_in, wu_in, wd_in,
    out_o, gtok_o, gg_o, gu_o, gd_o,
    xf, df, xs, ds_, wgf, wuf, wdf, wgh, wgl, wuh, wul, wdh, wdl,
    part, r1, r2, r3, r4, s1, s3, full,
    xt, xt_far, dy_far, ht, ht_far, far,
    xth, hth, bh, bl, dh, dl,
    op, rz, sz, rx,
    a_s, a_r, c_s, c_r, e_s, e_r, g_s, g_r, p_s, p_r, l_s,
):
    rep = lax.axis_index("rep")
    w = lax.axis_index("width")
    h = lax.axis_index("hid")
    y, xl = w // 2, w % 2
    z, xh = h // 2, h % 2

    def ydev(k):
        return (rep, ((y + k) % 4) * 2 + xl, h)

    xdev = (rep, y * 2 + (1 - xl), h)

    def zdev(k):
        return (rep, w, ((z + k) % 4) * 2 + xh)

    hdev = (rep, w, z * 2 + (1 - xh))
    pdev = (1 - rep, w, h)
    sent = []

    def send(src, dst, s, r, device):
        c = pltpu.make_async_remote_copy(
            src_ref=src, dst_ref=dst, send_sem=s, recv_sem=r,
            device_id=device, device_id_type=MESH,
        )
        c.start()
        sent.append(c)
        return c

    def local(src, dst, i):
        c = pltpu.make_async_copy(src, dst, l_s.at[i])
        c.start()
        return c

    def row8(k):
        return pl.ds(pl.multiple_of(8 * k, 8), 8)

    def arrived(copies):
        for d in copies:
            d.wait_recv()

    def ring(c, k=0):
        return pl.ds(pl.multiple_of(C * c + 16 * ((z + k) % 4), 16), 16)

    lx = local(tok_in, xf.at[ring(0)], 0)
    ly = local(cot_in, df.at[ring(0)], 1)
    lg = local(wg_in, wgf, 4)
    lu = local(wu_in, wuf, 5)
    ld = local(wd_in, wdf, 6)

    barrier = pltpu.get_barrier_semaphore()
    peers = [ydev(k) for k in (2, 1, 3)] + [xdev] + [zdev(k) for k in (2, 1, 3)] + [hdev] + [pdev]
    for d in peers:
        pl.semaphore_signal(barrier, inc=1, device_id=d, device_id_type=MESH)
    pl.semaphore_wait(barrier, len(peers))

    def spread(src, dst, i):
        out = [send(src, dst.at[ring(0)], a_s.at[i, k], a_r.at[i, k], zdev(k)) for k in (2, 1, 3)]
        out.append(send(src, dst.at[ring(1)], a_s.at[i, 0], a_r.at[i, 0], hdev))
        return out

    def spread_on(dst, i, first):
        arrived(first[3:])
        block = dst.at[ring(1)]
        return [send(block, block, a_s.at[i, 3 + k], a_r.at[i, 3 + k], zdev(k)) for k in (2, 1, 3)]

    ax = spread(tok_in, xf, 0)
    ad = spread(cot_in, df, 1)

    def halves(src, hi_ref, lo_ref):
        step = 32

        def body(i, _):
            at = pl.multiple_of(i * step, step)
            hi, lo = split(src[pl.ds(at, step), :])
            hi_ref[pl.ds(at, step), :] = hi
            lo_ref[pl.ds(at, step), :] = lo
            return 0

        lax.fori_loop(0, H // step, body, 0)

    def stacked(src, dst, c):
        hi, lo = split(src[pl.ds(C * c, C), :])
        dst[c, pl.ds(0, C), :] = hi
        dst[c, pl.ds(C, C), :] = lo

    def halved(v):
        return v.reshape(2, C // 2, v.shape[1])

    def scatter(c, g):
        lo, n = GROUPS[g]
        arrays = pl.ds(lo, n)
        out = [
            send(
                part.at[c, arrays, 1 - xl, :, SX], r1.at[c, arrays],
                c_s.at[c, g, 0], c_r.at[c, g, 0], xdev,
            )
        ]
        for k in (2, 1, 3):
            out.append(
                send(
                    part.at[c, arrays, :, row8((y + k) % 4), SY], r3.at[c, k - 1, arrays],
                    c_s.at[c, g, k], c_r.at[c, g, k], ydev(k),
                )
            )
        return out

    def scatter_on(c, g, first):
        lo, n = GROUPS[g]
        arrays = pl.ds(lo, n)
        arrived(first[:1])
        for a in range(lo, lo + n):
            s1[c, a] = part[c, a, xl, :, SX] + r1[c, a]
        out = []
        for k in (2, 1, 3):
            out.append(
                send(
                    s1.at[c, arrays, row8((y + k) % 4)], r2.at[c, k - 1, arrays],
                    c_s.at[c, g, 3 + k], c_r.at[c, g, 3 + k], ydev(k),
                )
            )
        arrived(first[1:])
        for a in range(lo, lo + n):
            s3[c, a] = part[c, a, :, row8(y), SY] + r3[c, 0, a] + r3[c, 1, a] + r3[c, 2, a]
        out.append(
            send(
                s3.at[c, arrays, 1 - xl], r4.at[c, arrays],
                c_s.at[c, g, 7], c_r.at[c, g, 7], xdev,
            )
        )
        return out

    def summed(c, a):
        left = s1[c, a, row8(y), :] + r2[c, 0, a] + r2[c, 1, a] + r2[c, 2, a]
        right = s3[c, a, xl] + r4[c, a]
        return jnp.concatenate([left, right], axis=1)

    def gather(c, g):
        lo, n = GROUPS_BACK[g]
        arrays = pl.ds(lo, n)
        mine = full.at[c, arrays, xl, row8(y), GY]
        out = [send(mine, mine, e_s.at[c, g, 0], e_r.at[c, g, 0], xdev)]
        mine = full.at[c, arrays, xl, row8(y), GX]
        for k in (2, 1, 3):
            out.append(send(mine, mine, e_s.at[c, g, k], e_r.at[c, g, k], ydev(k)))
        return out

    def gather_on(c, g, first):
        lo, n = GROUPS_BACK[g]
        arrays = pl.ds(lo, n)
        out = []
        arrived(first[:1])
        pair = full.at[c, arrays, :, row8(y), GY]
        for k in (2, 1, 3):
            out.append(send(pair, pair, e_s.at[c, g, 3 + k], e_r.at[c, g, 3 + k], ydev(k)))
        arrived(first[1:])
        half = full.at[c, arrays, xl, :, GX]
        out.append(send(half, half, e_s.at[c, g, 7], e_r.at[c, g, 7], xdev))
        return out

    def activate(c):
        gate = summed(c, 0)
        up = summed(c, 1)
        logistic = 1.0 / (1.0 + jnp.exp(-gate))
        full[c, 0, xl, row8(y), :] = gate * logistic * up
        return gather(c, 0), (gate, up, logistic)

    def derive(c, saved):
        gate, up, logistic = saved
        back = summed(c, 2)
        full[c, 1, xl, row8(y), :] = back * up * logistic * (1.0 + gate * (1.0 - logistic))
        full[c, 2, xl, row8(y), :] = back * gate * logistic
        return gather(c, 1)

    def whole(c, a):
        return full[c, a].reshape(C, HP)

    def reduce_rows(i, c):
        return [
            send(op.at[i, c, ring(0, k)], rz.at[i, c, k - 1], g_s.at[i, c, k], g_r.at[i, c, k], zdev(k))
            for k in (2, 1, 3)
        ]

    def ring_sum(i, c):
        return op[i, c, ring(0), :] + rz[i, c, 0] + rz[i, c, 1] + rz[i, c, 2]

    def reduce_on(i, first):
        arrived(first)
        sz[i] = ring_sum(i, 1)
        return [send(sz.at[i], rx.at[i], g_s.at[i, 0, 0], g_r.at[i, 0, 0], hdev)]

    def project(c):
        hi, lo = split(whole(c, 0))
        op[0, c] = dot3(jnp.concatenate([hi, lo], axis=0), wdh[...], wdl[...], NN)
        return reduce_rows(0, c)

    def pull_back(c):
        acc = None
        for i, (wh, wl) in enumerate(((wgh, wgl), (wuh, wul))):
            hi, lo = split(whole(c, 1 + i))
            bh[i, pl.ds(C * c, C), :] = hi
            bl[i, pl.ds(C * c, C), :] = lo
            term = dot3(jnp.concatenate([hi, lo], axis=0), wh[...], wl[...], NN)
            acc = term if acc is None else acc + term
        op[1, c] = acc
        return reduce_rows(1, c)

    def gate_up(c):
        arrived(kept.pop(("x", c)))
        stacked(xf, xs, c)
        part[c, 0] = halved(dot3(xs[c], wgh[...], wgl[...], NT))
        part[c, 1] = halved(dot3(xs[c], wuh[...], wul[...], NT))
        return scatter(c, 0)

    def back_part(c):
        arrived(kept.pop(("d", c)))
        stacked(df, ds_, c)
        part[c, 2] = halved(dot3(ds_[c], wdh[...], wdl[...], NT))
        return scatter(c, 1)

    for ref in (wgh, wgl, wuh, wul, wdh, wdl):
        ref[pl.ds(H, HP - H), :] = jnp.zeros((HP - H, W), BF16)
    lg.wait()
    halves(wgf, wgh, wgl)
    lu.wait()
    halves(wuf, wuh, wul)
    ld.wait()
    halves(wdf, wdh, wdl)
    lx.wait()
    ly.wait()
    kept = {("x", 0): ax[:3], ("d", 0): ad[:3]}

    def keep(name, value):
        kept[name] = value

    half_x = pl.multiple_of(320 * rep, 64)
    far_x = pl.multiple_of(320 * (1 - rep), 64)
    half_h = pl.multiple_of(432 * rep, 16)
    far_h = pl.multiple_of(432 * (1 - rep), 16)

    def do_activate(c):
        arrived(kept.pop(("d", c, 0)))
        copies, saved = activate(c)
        keep(("e", c, 0), copies)
        keep(("saved", c), saved)

    def do_derive(c):
        arrived(kept.pop(("d", c, 1)))
        keep(("e", c, 1), derive(c, kept.pop(("saved", c))))

    def do_project(c):
        arrived(kept.pop(("f", c, 0)))
        keep(("g", 0, c), project(c))

    def do_pull_back(c):
        arrived(kept.pop(("f", c, 1)))
        keep(("pg", c), send(full.at[c, pl.ds(1, 2)], far.at[c], p_s.at[3 + c], p_r.at[3 + c], pdev))
        keep(("g", 1, c), pull_back(c))

    def turn_tokens():
        for j in range(5):
            xt[pl.ds(128 * j, 128), :] = xf[:, pl.ds(128 * j, 128)].T
        keep("px", send(xt.at[pl.ds(far_x, 320)], xt_far, p_s.at[1], p_r.at[1], pdev))

    def turn_hidden():
        for j in range(7):
            lanes = pl.ds(128 * j, 128)
            block = [full[c, 0, :, :, lanes].reshape(C, 128) for c in range(2)]
            ht[pl.ds(128 * j, 128), :] = jnp.concatenate(block, axis=0).T
        keep("ph", send(ht.at[pl.ds(far_h, 432)], ht_far, p_s.at[2], p_r.at[2], pdev))

    steps = {
        "fx": lambda: keep(("x", 1), spread_on(xf, 0, ax)),
        "fd": lambda: keep(("d", 1), spread_on(df, 1, ad)),
        "dy": lambda: keep("py", send(df, dy_far, p_s.at[0], p_r.at[0], pdev)),
        "xt": turn_tokens,
        "ht": turn_hidden,
        "r01": lambda: keep(("g", 0), reduce_on(0, kept.pop(("g", 0, 1)))),
        "r11": lambda: keep(("g", 1), reduce_on(1, kept.pop(("g", 1, 1)))),
    }
    for c in range(2):
        steps[f"gu{c}"] = lambda c=c: keep(("c", c, 0), gate_up(c))
        steps[f"bk{c}"] = lambda c=c: keep(("c", c, 1), back_part(c))
        steps[f"act{c}"] = lambda c=c: do_activate(c)
        steps[f"der{c}"] = lambda c=c: do_derive(c)
        steps[f"pr{c}"] = lambda c=c: do_project(c)
        steps[f"pb{c}"] = lambda c=c: do_pull_back(c)
        for g in range(2):
            steps[f"s{c}{g}"] = lambda c=c, g=g: keep(("d", c, g), scatter_on(c, g, kept.pop(("c", c, g))))
            steps[f"f{c}{g}"] = lambda c=c, g=g: keep(("f", c, g), gather_on(c, g, kept.pop(("e", c, g))))
    for name in ORDER:
        steps[name]()

    kept["px"].wait_recv()
    for ref, at in ((xt.at[pl.ds(half_x, 320)], 0), (xt_far, ROWS)):
        hi, lo = split(ref[...])
        xth[pl.ds(0, 320), pl.ds(at, ROWS)] = hi
        xth[pl.ds(320, 320), pl.ds(at, ROWS)] = lo
    kept["py"].wait_recv()
    for c in range(2):
        dh[pl.ds(C * c, C), :] = ds_[c, pl.ds(0, C), :]
        dl[pl.ds(C * c, C), :] = ds_[c, pl.ds(C, C), :]
    hi, lo = split(dy_far[...])
    dh[pl.ds(ROWS, ROWS), :] = hi
    dl[pl.ds(ROWS, ROWS), :] = lo
    kept["ph"].wait_recv()
    for ref, at in ((ht.at[pl.ds(half_h, 432)], 0), (ht_far, ROWS)):
        hi, lo = split(ref[...])
        hth[pl.ds(0, 432), pl.ds(at, ROWS)] = hi
        hth[pl.ds(432, 432), pl.ds(at, ROWS)] = lo
    gd_o[...] = dot3(hth[...], dh[...], dl[...], NN)
    arrived([kept["pg", 0], kept["pg", 1]])
    for i, o in enumerate((gg_o, gu_o)):
        for c in range(2):
            hi, lo = split(far[c, i].reshape(C, HP))
            bh[i, pl.ds(ROWS + C * c, C), :] = hi
            bl[i, pl.ds(ROWS + C * c, C), :] = lo
        o[...] = dot3(xth[...], bh[i], bl[i], NN)[:, :H]

    for i, o in enumerate((out_o, gtok_o)):
        arrived(kept["g", i, 0])
        near = ring_sum(i, 0)
        arrived(kept["g", i])
        o[...] = near + rx[i]
    for c in sent:
        c.wait_send()


def write(*refs):
    copies = []
    for i in range(5):
        src, dst, sems = refs[i], refs[5 + i], refs[10]
        n = PIECES[i]
        rows = src.shape[0] // n
        for k in range(n):
            at = pl.ds(rows * k, rows)
            copies.append(pltpu.make_async_copy(src.at[at], dst.at[at], sems.at[i, k]))
    for c in copies:
        c.start()
    for c in copies:
        c.wait()


def shards(tokens, cotangent, w_gate, w_up, w_down):
    v = pltpu.VMEM
    dma = pltpu.SemaphoreType.DMA
    cy = HP - CX
    scratch = [
        v((ROWS, W), F32), v((ROWS, W), F32), v((2, 2 * C, W), BF16), v((2, 2 * C, W), BF16),
        *[v((H, W), F32)] * 3, *[v((HP, W), BF16)] * 6,
        v((2, 3, 2, 32, HP), F32), v((2, 3, 32, CX), F32), v((2, 3, 3, 8, CX), F32),
        v((2, 3, 3, 2, 8, cy), F32), v((2, 3, 8, cy), F32), v((2, 3, 32, CX), F32),
        v((2, 3, 2, 8, cy), F32), v((2, 3, 2, 32, HP), F32),
        v((W, ROWS), F32), v((320, ROWS), F32), v((ROWS, W), F32), v((HP, ROWS), F32), v((432, ROWS), F32),
        v((2, 2, 2, 32, HP), F32),
        v((640, 256), BF16), v((864, 256), BF16),
        v((2, 256, HP), BF16), v((2, 256, HP), BF16), v((256, W), BF16), v((256, W), BF16),
        v((2, 2, C, W), F32), v((2, 2, 3, 16, W), F32), v((2, 16, W), F32), v((2, 16, W), F32),
        dma((2, 7)), dma((2, 7)), dma((2, 2, 8)), dma((2, 2, 8)), dma((2, 2, 8)), dma((2, 2, 8)),
        dma((2, 2, 4)), dma((2, 2, 4)), dma((5,)), dma((5,)), dma((7,)),
    ]
    any_ = pl.BlockSpec(memory_space=pl.ANY)
    vmem = pl.BlockSpec(memory_space=pltpu.VMEM)
    hbm = pl.BlockSpec(memory_space=pltpu.HBM)
    shapes = [(16, W), (16, W), (320, H), (320, H), (432, W)]
    results = pl.pallas_call(
        kernel,
        out_shape=[v(s, F32) for s in shapes],
        in_specs=[hbm] * 5,
        out_specs=[vmem] * 5,
        scratch_shapes=scratch,
        compiler_params=pltpu.CompilerParams(
            collective_id=0, has_side_effects=True, vmem_limit_bytes=48 << 20
        ),
    )(*[pltpu.with_memory_space_constraint(a, pltpu.HBM) for a in (tokens, cotangent, w_gate.T, w_up.T, w_down)])
    results = [pltpu.with_memory_space_constraint(r, pltpu.VMEM) for r in results]
    out, gtok, gg, gu, gd = pl.pallas_call(
        write,
        out_shape=[jax.ShapeDtypeStruct(s, F32) for s in shapes],
        in_specs=[vmem] * 5,
        out_specs=[any_] * 5,
        scratch_shapes=[dma((5, max(PIECES)))],
    )(*results)
    return out, gtok, gg[None, None], gu[None, None], gd[None, None]


def solution(mesh):
    return jax.shard_map(
        shards,
        mesh=mesh,
        in_specs=(
            P(("rep", "hid"), "width"), P(("rep", "hid"), "width"),
            P("width", "hid"), P("width", "hid"), P("hid", "width"),
        ),
        out_specs=(
            P(("rep", "hid"), "width"), P(("rep", "hid"), "width"),
            P("width", "rep", None, "hid"), P("width", "rep", None, "hid"),
            P("hid", "rep", None, "width"),
        ),
        check_vma=False,
    )
```

```python
import functools

import jax
import jax.numpy as jnp
from jax import lax
from jax.experimental import pallas as pl
from jax.experimental.pallas import tpu as pltpu
from jax.sharding import PartitionSpec as P

MESH = pl.DeviceIdType.MESH
F32 = jnp.float32
BF16 = jnp.bfloat16
NN = (((1,), (0,)), ((), ()))
ROWS = 128
W = 640
H = 864
HP = 896
C = 64
CX = 512
EX = 384
SX, SY = pl.ds(0, CX), pl.ds(CX, HP - CX)
GX, GY = pl.ds(0, EX), pl.ds(EX, HP - EX)
GROUPS = ((0, 1), (1, 1), (2, 1))
COLUMNS = (pl.ds(0, 640),)
FAR_DIRECT = True
GROUPS_BACK = ((0, 1), (1, 2))
PIECES = (1, 1, 1, 1, 1)
ORDER = (
    "fx", "gu0", "fd", "bk0", "gu1", "bk1", "s00", "s01", "s02", "s10", "s11", "s12", "act0", "dy", "der0",
    "act1", "der1", "f00", "xt", "f10", "f11", "f01", "pr0", "pr1", "tt", "ht", "pb1", "gd", "pb0", "r01", "gw",
)


def split(v):
    hi = v.astype(BF16)
    return hi, (v - hi.astype(F32)).astype(BF16)


def dot(a, b, dims):
    return lax.dot_general(a, b, dims, preferred_element_type=F32)


def dot3(stack, b_hi, b_lo, dims):
    m = stack.shape[0] // 2
    both = dot(stack, b_hi, dims)
    return both[:m] + both[m:] + dot(stack[:m], b_lo, dims)


def kernel(
    tok_in, cot_in, wg_in, wu_in, wd_in,
    out_o, gtok_o, gg_o, gu_o, gd_o,
    xf, df, xs, ds_, wgf, wuf, wdf, wgh, wgl, wuh, wul, wdh, wdl,
    wgth, wgtl, wuth, wutl, wdth, wdtl,
    part, r1, r2, r3, r4, s1, s3, full,
    xt, xt_far, dy_far, ht, ht_far, far,
    xth, hth, bh, bl, dh, dl,
    op, rz, sz, rx, rf,
    a_s, a_r, c_s, c_r, e_s, e_r, g_s, g_r, p_s, p_r, l_s,
):
    rep = lax.axis_index("rep")
    w = lax.axis_index("width")
    h = lax.axis_index("hid")
    y, xl = w // 2, w % 2
    z, xh = h // 2, h % 2

    def ydev(k):
        return (rep, ((y + k) % 4) * 2 + xl, h)

    xdev = (rep, y * 2 + (1 - xl), h)

    def zdev(k):
        return (rep, w, ((z + k) % 4) * 2 + xh)

    def odev(k):
        return (rep, w, ((z + k) % 4) * 2 + (1 - xh))

    hdev = odev(0)
    pdev = (1 - rep, w, h)
    sent = []

    def send(src, dst, s, r, device):
        c = pltpu.make_async_remote_copy(
            src_ref=src, dst_ref=dst, send_sem=s, recv_sem=r,
            device_id=device, device_id_type=MESH,
        )
        c.start()
        sent.append(c)
        return c

    def local(src, dst, i):
        c = pltpu.make_async_copy(src, dst, l_s.at[i])
        c.start()
        return c

    def row8(k):
        return pl.ds(pl.multiple_of(8 * k, 8), 8)

    def arrived(copies):
        for d in copies:
            d.wait_recv()

    def ring(c, k=0):
        return pl.ds(pl.multiple_of(C * c + 16 * ((z + k) % 4), 16), 16)

    lx = local(tok_in, xf.at[ring(0)], 0)
    ly = local(cot_in, df.at[ring(0)], 1)
    lg = local(wg_in, wgf.at[pl.ds(0, H)], 2)
    lu = local(wu_in, wuf.at[pl.ds(0, H)], 3)
    ld = local(wd_in, wdf.at[pl.ds(0, H)], 4)
    for ref in (wgf, wuf, wdf):
        ref[pl.ds(H, HP - H), :] = jnp.zeros((HP - H, W), F32)

    barrier = pltpu.get_barrier_semaphore()
    peers = [ydev(k) for k in (2, 1, 3)] + [xdev] + [zdev(k) for k in (2, 1, 3)] + [hdev] + [pdev]
    for d in peers:
        pl.semaphore_signal(barrier, inc=1, device_id=d, device_id_type=MESH)
    pl.semaphore_wait(barrier, len(peers))

    def spread(src, dst, i):
        out = [send(src, dst.at[ring(0)], a_s.at[i, k], a_r.at[i, k], zdev(k)) for k in (2, 1, 3)]
        out.append(send(src, dst.at[ring(1)], a_s.at[i, 0], a_r.at[i, 0], hdev))
        return out

    def spread_on(dst, i, first):
        arrived(first[3:])
        block = dst.at[ring(1)]
        return [send(block, block, a_s.at[i, 3 + k], a_r.at[i, 3 + k], zdev(k)) for k in (2, 1, 3)]

    ax = spread(tok_in, xf, 0)
    ad = spread(cot_in, df, 1)

    def halves(src, hi_ref, lo_ref, turned_hi, turned_lo):
        def body(i, _):
            at = pl.ds(pl.multiple_of(i * 128, 128), 128)
            v = src[at, :]
            hi_ref[at, :], lo_ref[at, :] = split(v)
            turned_hi[:, at], turned_lo[:, at] = split(v.T)
            return 0

        lax.fori_loop(0, HP // 128, body, 0)

    def stacked(src, dst, c):
        hi, lo = split(src[pl.ds(C * c, C), :])
        dst[c, pl.ds(0, C), :] = hi
        dst[c, pl.ds(C, C), :] = lo

    def halved(v):
        return v.reshape(2, C // 2, v.shape[1])

    def scatter(c, g):
        lo, n = GROUPS[g]
        arrays = pl.ds(lo, n)
        out = [
            send(
                part.at[c, arrays, 1 - xl, :, SX], r1.at[c, arrays],
                c_s.at[c, g, 0], c_r.at[c, g, 0], xdev,
            )
        ]
        for k in (2, 1, 3):
            out.append(
                send(
                    part.at[c, arrays, :, row8((y + k) % 4), SY], r3.at[c, k - 1, arrays],
                    c_s.at[c, g, k], c_r.at[c, g, k], ydev(k),
                )
            )
        return out

    def scatter_on(c, g, first):
        lo, n = GROUPS[g]
        arrays = pl.ds(lo, n)
        arrived(first[:1])
        for a in range(lo, lo + n):
            s1[c, a] = part[c, a, xl, :, SX] + r1[c, a]
        out = []
        for k in (2, 1, 3):
            out.append(
                send(
                    s1.at[c, arrays, row8((y + k) % 4)], r2.at[c, k - 1, arrays],
                    c_s.at[c, g, 3 + k], c_r.at[c, g, 3 + k], ydev(k),
                )
            )
        arrived(first[1:])
        for a in range(lo, lo + n):
            s3[c, a] = part[c, a, :, row8(y), SY] + r3[c, 0, a] + r3[c, 1, a] + r3[c, 2, a]
        out.append(
            send(
                s3.at[c, arrays, 1 - xl], r4.at[c, arrays],
                c_s.at[c, g, 7], c_r.at[c, g, 7], xdev,
            )
        )
        return out

    def summed(c, a):
        left = s1[c, a, row8(y), :] + r2[c, 0, a] + r2[c, 1, a] + r2[c, 2, a]
        right = s3[c, a, xl] + r4[c, a]
        return jnp.concatenate([left, right], axis=1)

    def gather(c, g):
        lo, n = GROUPS_BACK[g]
        arrays = pl.ds(lo, n)
        mine = full.at[c, arrays, xl, row8(y), GY]
        out = [send(mine, mine, e_s.at[c, g, 0], e_r.at[c, g, 0], xdev)]
        mine = full.at[c, arrays, xl, row8(y), GX]
        for k in (2, 1, 3):
            out.append(send(mine, mine, e_s.at[c, g, k], e_r.at[c, g, k], ydev(k)))
        return out

    def gather_on(c, g, first):
        lo, n = GROUPS_BACK[g]
        arrays = pl.ds(lo, n)
        out = []
        arrived(first[:1])
        pair = full.at[c, arrays, :, row8(y), GY]
        for k in (2, 1, 3):
            out.append(send(pair, pair, e_s.at[c, g, 3 + k], e_r.at[c, g, 3 + k], ydev(k)))
        arrived(first[1:])
        half = full.at[c, arrays, xl, :, GX]
        out.append(send(half, half, e_s.at[c, g, 7], e_r.at[c, g, 7], xdev))
        return out

    def activate(c):
        gate = summed(c, 0)
        up = summed(c, 1)
        logistic = 1.0 / (1.0 + jnp.exp(-gate))
        full[c, 0, xl, row8(y), :] = gate * logistic * up
        return gather(c, 0), (gate, up, logistic)

    def derive(c, saved):
        gate, up, logistic = saved
        back = summed(c, 2)
        full[c, 1, xl, row8(y), :] = back * up * logistic * (1.0 + gate * (1.0 - logistic))
        full[c, 2, xl, row8(y), :] = back * gate * logistic
        return gather(c, 1)

    def whole(c, a):
        return full[c, a].reshape(C, HP)

    def reduce_rows(i, c, cols, part_no):
        return [
            send(
                op.at[i, c, ring(0, k), cols], rz.at[i, c, k - 1, :, cols],
                g_s.at[i, c, part_no, k], g_r.at[i, c, part_no, k], zdev(k),
            )
            for k in (2, 1, 3)
        ]

    def ring_sum(i, c):
        return op[i, c, ring(0), :] + rz[i, c, 0] + rz[i, c, 1] + rz[i, c, 2]

    def reduce_far(i, cols, part_no):
        return [
            send(
                op.at[i, 1, ring(0, k), cols], rf.at[k, :, cols],
                g_s.at[i, 1, part_no, k], g_r.at[i, 1, part_no, k], odev(k),
            )
            for k in (2, 1, 3, 0)
        ]

    def reduce_on(i, first):
        arrived(first)
        sz[i] = ring_sum(i, 1)
        return [send(sz.at[i], rx.at[i], g_s.at[i, 0, 0, 0], g_r.at[i, 0, 0, 0], hdev)]

    def project(c):
        hi, lo = split(whole(c, 0))
        op[0, c] = dot3(jnp.concatenate([hi, lo], axis=0), wdh[...], wdl[...], NN)
        return reduce_rows(0, c, pl.ds(0, W), 0)

    def pull_back(c):
        terms = []
        for i in range(2):
            at = pl.ds(C * c, C)
            hi, lo = split(whole(c, 1 + i))
            bh[i, at, :], bl[i, at, :] = hi, lo
            terms.append(jnp.concatenate([hi, lo], axis=0))
        copies = []
        for part_no, cols in enumerate(COLUMNS):
            op[1, c, :, cols] = dot3(terms[0], wgh[:, cols], wgl[:, cols], NN) + dot3(terms[1], wuh[:, cols], wul[:, cols], NN)
            if c == 1 and FAR_DIRECT:
                copies += reduce_far(1, cols, part_no)
            else:
                copies += reduce_rows(1, c, cols, part_no)
        return copies

    def gate_up(c):
        arrived(kept.pop(("x", c)))
        stacked(xf, xs, c)
        part[c, 0] = halved(dot3(xs[c], wgth[...], wgtl[...], NN))
        gate = scatter(c, 0)
        part[c, 1] = halved(dot3(xs[c], wuth[...], wutl[...], NN))
        return gate, scatter(c, 1)

    def back_part(c):
        arrived(kept.pop(("d", c)))
        stacked(df, ds_, c)
        part[c, 2] = halved(dot3(ds_[c], wdth[...], wdtl[...], NN))
        return scatter(c, 2)

    lg.wait()
    halves(wgf, wgh, wgl, wgth, wgtl)
    lu.wait()
    halves(wuf, wuh, wul, wuth, wutl)
    ld.wait()
    halves(wdf, wdh, wdl, wdth, wdtl)
    lx.wait()
    ly.wait()
    kept = {("x", 0): ax[:3], ("d", 0): ad[:3]}

    def keep(name, value):
        kept[name] = value

    half_x = pl.multiple_of(320 * rep, 64)
    far_x = pl.multiple_of(320 * (1 - rep), 64)
    half_h = pl.multiple_of(432 * rep, 16)
    far_h = pl.multiple_of(432 * (1 - rep), 16)

    def do_gate_up(c):
        kept["c", c, 0], kept["c", c, 1] = gate_up(c)

    def do_activate(c):
        arrived(kept.pop(("d", c, 0)) + kept.pop(("d", c, 1)))
        copies, saved = activate(c)
        keep(("e", c, 0), copies)
        keep(("saved", c), saved)

    def do_derive(c):
        arrived(kept.pop(("d", c, 2)))
        keep(("e", c, 1), derive(c, kept.pop(("saved", c))))

    def do_project(c):
        arrived(kept.pop(("f", c, 0)))
        keep(("g", 0, c), project(c))

    def do_pull_back(c):
        arrived(kept.pop(("f", c, 1)))
        keep(("pg", c), send(full.at[c, pl.ds(1, 2)], far.at[c], p_s.at[3 + c], p_r.at[3 + c], pdev))
        keep(("g", 1, c), pull_back(c))

    def turn_tokens():
        for j in range(5):
            xt[pl.ds(128 * j, 128), :] = xf[:, pl.ds(128 * j, 128)].T
        keep("px", send(xt.at[pl.ds(far_x, 320)], xt_far, p_s.at[1], p_r.at[1], pdev))

    def turn_hidden():
        for j in range(7):
            lanes = pl.ds(128 * j, 128)
            block = [full[c, 0, :, :, lanes].reshape(C, 128) for c in range(2)]
            ht[pl.ds(128 * j, 128), :] = jnp.concatenate(block, axis=0).T
        keep("ph", send(ht.at[pl.ds(far_h, 432)], ht_far, p_s.at[2], p_r.at[2], pdev))

    steps = {
        "fx": lambda: keep(("x", 1), spread_on(xf, 0, ax)),
        "fd": lambda: keep(("d", 1), spread_on(df, 1, ad)),
        "dy": lambda: keep("py", send(df, dy_far, p_s.at[0], p_r.at[0], pdev)),
        "xt": turn_tokens,
        "ht": turn_hidden,
        "r01": lambda: keep(("g", 0), reduce_on(0, kept.pop(("g", 0, 1)))),
        "r11": lambda: keep(("g", 1), reduce_on(1, kept.pop(("g", 1, 1)))),
    }
    for c in range(2):
        steps[f"gu{c}"] = lambda c=c: do_gate_up(c)
        steps[f"bk{c}"] = lambda c=c: keep(("c", c, 2), back_part(c))
        steps[f"act{c}"] = lambda c=c: do_activate(c)
        steps[f"der{c}"] = lambda c=c: do_derive(c)
        steps[f"pr{c}"] = lambda c=c: do_project(c)
        steps[f"pb{c}"] = lambda c=c: do_pull_back(c)
        for g in range(3):
            steps[f"s{c}{g}"] = lambda c=c, g=g: keep(("d", c, g), scatter_on(c, g, kept.pop(("c", c, g))))
        for g in range(2):
            steps[f"f{c}{g}"] = lambda c=c, g=g: keep(("f", c, g), gather_on(c, g, kept.pop(("e", c, g))))
    def token_terms():
        arrived([kept["px"], kept["py"]])
        for ref, at in ((xt.at[pl.ds(half_x, 320)], 0), (xt_far, ROWS)):
            hi, lo = split(ref[...])
            xth[pl.ds(0, 320), pl.ds(at, ROWS)] = hi
            xth[pl.ds(320, 320), pl.ds(at, ROWS)] = lo
        for c in range(2):
            dh[pl.ds(C * c, C), :] = ds_[c, pl.ds(0, C), :]
            dl[pl.ds(C * c, C), :] = ds_[c, pl.ds(C, C), :]
        dh[pl.ds(ROWS, ROWS), :], dl[pl.ds(ROWS, ROWS), :] = split(dy_far[...])

    def down_gradient():
        arrived([kept["ph"]])
        for ref, at in ((ht.at[pl.ds(half_h, 432)], 0), (ht_far, ROWS)):
            hi, lo = split(ref[...])
            hth[pl.ds(0, 432), pl.ds(at, ROWS)] = hi
            hth[pl.ds(432, 432), pl.ds(at, ROWS)] = lo
        gd_o[...] = dot3(hth[...], dh[...], dl[...], NN)

    def gate_up_gradients():
        arrived([kept["pg", 0], kept["pg", 1]])
        for i, o in enumerate((gg_o, gu_o)):
            for c in range(2):
                at = pl.ds(ROWS + C * c, C)
                bh[i, at, :], bl[i, at, :] = split(far[c, i].reshape(C, HP))
            o[...] = dot3(xth[...], bh[i], bl[i], NN)[:, :H]

    steps["tt"] = token_terms
    steps["gd"] = down_gradient
    steps["gw"] = gate_up_gradients
    for name in ORDER:
        steps[name]()

    arrived(kept["g", 0, 0] + kept["g", 0])
    out_o[...] = ring_sum(0, 0) + rx[0]
    arrived(kept["g", 1, 0])
    near = ring_sum(1, 0)
    if FAR_DIRECT:
        arrived(kept["g", 1, 1])
        gtok_o[...] = near + rf[0] + rf[1] + rf[2] + rf[3]
    else:
        arrived(kept["g", 1])
        gtok_o[...] = near + rx[1]
    for c in sent:
        c.wait_send()


def write(*refs):
    copies = []
    for i in range(5):
        src, dst, sems = refs[i], refs[5 + i], refs[10]
        n = PIECES[i]
        rows = src.shape[0] // n
        for k in range(n):
            at = pl.ds(rows * k, rows)
            copies.append(pltpu.make_async_copy(src.at[at], dst.at[at], sems.at[i, k]))
    for c in copies:
        c.start()
    for c in copies:
        c.wait()


def shards(tokens, cotangent, w_gate, w_up, w_down):
    v = pltpu.VMEM
    dma = pltpu.SemaphoreType.DMA
    cy = HP - CX
    scratch = [
        v((ROWS, W), F32), v((ROWS, W), F32), v((2, 2 * C, W), BF16), v((2, 2 * C, W), BF16),
        *[v((HP, W), F32)] * 3, *[v((HP, W), BF16)] * 6, *[v((W, HP), BF16)] * 6,
        v((2, 3, 2, 32, HP), F32), v((2, 3, 32, CX), F32), v((2, 3, 3, 8, CX), F32),
        v((2, 3, 3, 2, 8, cy), F32), v((2, 3, 8, cy), F32), v((2, 3, 32, CX), F32),
        v((2, 3, 2, 8, cy), F32), v((2, 3, 2, 32, HP), F32),
        v((W, ROWS), F32), v((320, ROWS), F32), v((ROWS, W), F32), v((HP, ROWS), F32), v((432, ROWS), F32),
        v((2, 2, 2, 32, HP), F32),
        v((640, 256), BF16), v((864, 256), BF16),
        v((2, 256, HP), BF16), v((2, 256, HP), BF16), v((256, W), BF16), v((256, W), BF16),
        v((2, 2, C, W), F32), v((2, 2, 3, 16, W), F32), v((2, 16, W), F32), v((2, 16, W), F32), v((4, 16, W), F32),
        dma((2, 7)), dma((2, 7)), dma((2, 3, 8)), dma((2, 3, 8)), dma((2, 2, 8)), dma((2, 2, 8)),
        dma((2, 2, 2, 4)), dma((2, 2, 2, 4)), dma((5,)), dma((5,)), dma((5,)),
    ]
    any_ = pl.BlockSpec(memory_space=pl.ANY)
    vmem = pl.BlockSpec(memory_space=pltpu.VMEM)
    hbm = pl.BlockSpec(memory_space=pltpu.HBM)
    shapes = [(16, W), (16, W), (320, H), (320, H), (432, W)]
    results = pl.pallas_call(
        kernel,
        out_shape=[v(s, F32) for s in shapes],
        in_specs=[hbm] * 5,
        out_specs=[vmem] * 5,
        scratch_shapes=scratch,
        compiler_params=pltpu.CompilerParams(
            collective_id=0, has_side_effects=True, vmem_limit_bytes=48 << 20
        ),
    )(*[pltpu.with_memory_space_constraint(a, pltpu.HBM) for a in (tokens, cotangent, w_gate.T, w_up.T, w_down)])
    results = [pltpu.with_memory_space_constraint(r, pltpu.VMEM) for r in results]
    out, gtok, gg, gu, gd = pl.pallas_call(
        write,
        out_shape=[jax.ShapeDtypeStruct(s, F32) for s in shapes],
        in_specs=[vmem] * 5,
        out_specs=[any_] * 5,
        scratch_shapes=[dma((5, max(PIECES)))],
    )(*results)
    return out, gtok, gg[None, None], gu[None, None], gd[None, None]


def solution(mesh):
    return jax.shard_map(
        shards,
        mesh=mesh,
        in_specs=(
            P(("rep", "hid"), "width"), P(("rep", "hid"), "width"),
            P("width", "hid"), P("width", "hid"), P("hid", "width"),
        ),
        out_specs=(
            P(("rep", "hid"), "width"), P(("rep", "hid"), "width"),
            P("width", "rep", None, "hid"), P("width", "rep", None, "hid"),
            P("hid", "rep", None, "width"),
        ),
        check_vma=False,
    )
```

```python
import functools

import jax
import jax.numpy as jnp
from jax import lax
from jax.experimental import pallas as pl
from jax.experimental.pallas import tpu as pltpu
from jax.sharding import PartitionSpec as P

MESH = pl.DeviceIdType.MESH
F32 = jnp.float32
BF16 = jnp.bfloat16
NN = (((1,), (0,)), ((), ()))
ROWS = 128
W = 640
H = 864
HP = 896
C = 64
CX = 512
EX = (512, 384)
SX, SY = pl.ds(0, CX), pl.ds(CX, HP - CX)
GX = [pl.ds(0, e) for e in EX]
GY = [pl.ds(e, HP - e) for e in EX]
GROUPS = ((0, 1), (1, 1), (2, 1))
COLUMNS = (pl.ds(0, 640),)
FAR_DIRECT = True
GROUPS_BACK = ((0, 1), (1, 2))
PIECES = (1, 1, 1, 1, 1)
ORDER = ("fx", "gu0", "fd", "bk0", "gu1", "s00", "s01", "bk1", "s02", "s10", "s11", "s12", "act0", "dy", "der0", "act1", "der1", "f00", "xt", "f10", "f11", "f01", "pr0", "pr1", "tt", "ht", "pb1", "gd", "pb0", "r01", "gw")


def split(v):
    hi = v.astype(BF16)
    return hi, (v - hi.astype(F32)).astype(BF16)


def dot(a, b, dims):
    return lax.dot_general(a, b, dims, preferred_element_type=F32)


def dot3(stack, b_hi, b_lo, dims):
    m = stack.shape[0] // 2
    both = dot(stack, b_hi, dims)
    return both[:m] + both[m:] + dot(stack[:m], b_lo, dims)


def kernel(
    tok_in, cot_in, wg_in, wu_in, wd_in,
    out_o, gtok_o, gg_o, gu_o, gd_o,
    xf, df, xs, ds_, wgf, wuf, wdf, wgh, wgl, wuh, wul, wdh, wdl,
    wgth, wgtl, wuth, wutl, wdth, wdtl,
    part, r1, r2, r3, r4, s1, s3, full,
    xt, xt_far, dy_far, ht, ht_far, far,
    xth, hth, bh, bl, dh, dl,
    op, rz, sz, rx, rf,
    a_s, a_r, c_s, c_r, e_s, e_r, g_s, g_r, p_s, p_r, l_s,
):
    rep = lax.axis_index("rep")
    w = lax.axis_index("width")
    h = lax.axis_index("hid")
    y, xl = w // 2, w % 2
    z, xh = h // 2, h % 2

    def ydev(k):
        return (rep, ((y + k) % 4) * 2 + xl, h)

    xdev = (rep, y * 2 + (1 - xl), h)

    def zdev(k):
        return (rep, w, ((z + k) % 4) * 2 + xh)

    def odev(k):
        return (rep, w, ((z + k) % 4) * 2 + (1 - xh))

    hdev = odev(0)
    pdev = (1 - rep, w, h)
    sent = []

    def send(src, dst, s, r, device):
        c = pltpu.make_async_remote_copy(
            src_ref=src, dst_ref=dst, send_sem=s, recv_sem=r,
            device_id=device, device_id_type=MESH,
        )
        c.start()
        sent.append(c)
        return c

    def local(src, dst, i):
        c = pltpu.make_async_copy(src, dst, l_s.at[i])
        c.start()
        return c

    def row8(k):
        return pl.ds(pl.multiple_of(8 * k, 8), 8)

    def arrived(copies):
        for d in copies:
            d.wait_recv()

    def ring(c, k=0):
        return pl.ds(pl.multiple_of(C * c + 16 * ((z + k) % 4), 16), 16)

    lx = local(tok_in, xf.at[ring(0)], 0)
    ly = local(cot_in, df.at[ring(0)], 1)
    lg = local(wg_in, wgf.at[pl.ds(0, H)], 2)
    lu = local(wu_in, wuf.at[pl.ds(0, H)], 3)
    ld = local(wd_in, wdf.at[pl.ds(0, H)], 4)
    for ref in (wgf, wuf, wdf):
        ref[pl.ds(H, HP - H), :] = jnp.zeros((HP - H, W), F32)

    barrier = pltpu.get_barrier_semaphore()
    peers = [ydev(k) for k in (2, 1, 3)] + [xdev] + [zdev(k) for k in (2, 1, 3)] + [hdev] + [pdev]
    for d in peers:
        pl.semaphore_signal(barrier, inc=1, device_id=d, device_id_type=MESH)
    pl.semaphore_wait(barrier, len(peers))

    def spread(src, dst, i):
        out = [send(src, dst.at[ring(0)], a_s.at[i, k], a_r.at[i, k], zdev(k)) for k in (2, 1, 3)]
        out.append(send(src, dst.at[ring(1)], a_s.at[i, 0], a_r.at[i, 0], hdev))
        return out

    def spread_on(dst, i, first):
        arrived(first[3:])
        block = dst.at[ring(1)]
        return [send(block, block, a_s.at[i, 3 + k], a_r.at[i, 3 + k], zdev(k)) for k in (2, 1, 3)]

    ax = spread(tok_in, xf, 0)
    ad = spread(cot_in, df, 1)

    def halves(src, hi_ref, lo_ref, turned_hi, turned_lo):
        def body(i, _):
            at = pl.ds(pl.multiple_of(i * 128, 128), 128)
            v = src[at, :]
            hi_ref[at, :], lo_ref[at, :] = split(v)
            turned_hi[:, at], turned_lo[:, at] = split(v.T)
            return 0

        lax.fori_loop(0, HP // 128, body, 0)

    def stacked(src, dst, c):
        hi, lo = split(src[pl.ds(C * c, C), :])
        dst[c, pl.ds(0, C), :] = hi
        dst[c, pl.ds(C, C), :] = lo

    def halved(v):
        return v.reshape(2, C // 2, v.shape[1])

    def scatter(c, g):
        lo, n = GROUPS[g]
        arrays = pl.ds(lo, n)
        out = [
            send(
                part.at[c, arrays, 1 - xl, :, SX], r1.at[c, arrays],
                c_s.at[c, g, 0], c_r.at[c, g, 0], xdev,
            )
        ]
        for k in (2, 1, 3):
            out.append(
                send(
                    part.at[c, arrays, :, row8((y + k) % 4), SY], r3.at[c, k - 1, arrays],
                    c_s.at[c, g, k], c_r.at[c, g, k], ydev(k),
                )
            )
        return out

    def scatter_on(c, g, first):
        lo, n = GROUPS[g]
        arrays = pl.ds(lo, n)
        arrived(first[:1])
        for a in range(lo, lo + n):
            s1[c, a] = part[c, a, xl, :, SX] + r1[c, a]
        out = []
        for k in (2, 1, 3):
            out.append(
                send(
                    s1.at[c, arrays, row8((y + k) % 4)], r2.at[c, k - 1, arrays],
                    c_s.at[c, g, 3 + k], c_r.at[c, g, 3 + k], ydev(k),
                )
            )
        arrived(first[1:])
        for a in range(lo, lo + n):
            s3[c, a] = part[c, a, :, row8(y), SY] + r3[c, 0, a] + r3[c, 1, a] + r3[c, 2, a]
        out.append(
            send(
                s3.at[c, arrays, 1 - xl], r4.at[c, arrays],
                c_s.at[c, g, 7], c_r.at[c, g, 7], xdev,
            )
        )
        return out

    def summed(c, a):
        left = s1[c, a, row8(y), :] + r2[c, 0, a] + r2[c, 1, a] + r2[c, 2, a]
        right = s3[c, a, xl] + r4[c, a]
        return jnp.concatenate([left, right], axis=1)

    def gather(c, g):
        lo, n = GROUPS_BACK[g]
        arrays = pl.ds(lo, n)
        mine = full.at[c, arrays, xl, row8(y), GY[g]]
        out = [send(mine, mine, e_s.at[c, g, 0], e_r.at[c, g, 0], xdev)]
        mine = full.at[c, arrays, xl, row8(y), GX[g]]
        for k in (2, 1, 3):
            out.append(send(mine, mine, e_s.at[c, g, k], e_r.at[c, g, k], ydev(k)))
        return out

    def gather_on(c, g, first):
        lo, n = GROUPS_BACK[g]
        arrays = pl.ds(lo, n)
        out = []
        arrived(first[:1])
        pair = full.at[c, arrays, :, row8(y), GY[g]]
        for k in (2, 1, 3):
            out.append(send(pair, pair, e_s.at[c, g, 3 + k], e_r.at[c, g, 3 + k], ydev(k)))
        arrived(first[1:])
        half = full.at[c, arrays, xl, :, GX[g]]
        out.append(send(half, half, e_s.at[c, g, 7], e_r.at[c, g, 7], xdev))
        return out

    def activate(c):
        gate = summed(c, 0)
        up = summed(c, 1)
        logistic = 1.0 / (1.0 + jnp.exp(-gate))
        full[c, 0, xl, row8(y), :] = gate * logistic * up
        return gather(c, 0), (gate, up, logistic)

    def derive(c, saved):
        gate, up, logistic = saved
        back = summed(c, 2)
        full[c, 1, xl, row8(y), :] = back * up * logistic * (1.0 + gate * (1.0 - logistic))
        full[c, 2, xl, row8(y), :] = back * gate * logistic
        return gather(c, 1)

    def whole(c, a):
        return full[c, a].reshape(C, HP)

    def reduce_rows(i, c, cols, part_no):
        return [
            send(
                op.at[i, c, ring(0, k), cols], rz.at[i, c, k - 1, :, cols],
                g_s.at[i, c, part_no, k], g_r.at[i, c, part_no, k], zdev(k),
            )
            for k in (2, 1, 3)
        ]

    def ring_sum(i, c):
        return op[i, c, ring(0), :] + rz[i, c, 0] + rz[i, c, 1] + rz[i, c, 2]

    def reduce_far(i, cols, part_no):
        return [
            send(
                op.at[i, 1, ring(0, k), cols], rf.at[k, :, cols],
                g_s.at[i, 1, part_no, k], g_r.at[i, 1, part_no, k], odev(k),
            )
            for k in (0, 2, 1, 3)
        ]

    def reduce_on(i, first):
        arrived(first)
        sz[i] = ring_sum(i, 1)
        return [send(sz.at[i], rx.at[i], g_s.at[i, 0, 0, 0], g_r.at[i, 0, 0, 0], hdev)]

    def project(c):
        hi, lo = split(whole(c, 0))
        op[0, c] = dot3(jnp.concatenate([hi, lo], axis=0), wdh[...], wdl[...], NN)
        return reduce_rows(0, c, pl.ds(0, W), 0)

    def pull_back(c):
        terms = []
        for i in range(2):
            at = pl.ds(C * c, C)
            hi, lo = split(whole(c, 1 + i))
            bh[i, at, :], bl[i, at, :] = hi, lo
            terms.append(jnp.concatenate([hi, lo], axis=0))
        copies = []
        for part_no, cols in enumerate(COLUMNS):
            op[1, c, :, cols] = dot3(terms[0], wgh[:, cols], wgl[:, cols], NN) + dot3(terms[1], wuh[:, cols], wul[:, cols], NN)
            if c == 1 and FAR_DIRECT:
                copies += reduce_far(1, cols, part_no)
            else:
                copies += reduce_rows(1, c, cols, part_no)
        return copies

    def gate_up(c):
        arrived(kept.pop(("x", c)))
        stacked(xf, xs, c)
        part[c, 0] = halved(dot3(xs[c], wgth[...], wgtl[...], NN))
        gate = scatter(c, 0)
        part[c, 1] = halved(dot3(xs[c], wuth[...], wutl[...], NN))
        return gate, scatter(c, 1)

    def back_part(c):
        arrived(kept.pop(("d", c)))
        stacked(df, ds_, c)
        part[c, 2] = halved(dot3(ds_[c], wdth[...], wdtl[...], NN))
        return scatter(c, 2)

    lg.wait()
    halves(wgf, wgh, wgl, wgth, wgtl)
    lu.wait()
    halves(wuf, wuh, wul, wuth, wutl)
    ld.wait()
    halves(wdf, wdh, wdl, wdth, wdtl)
    lx.wait()
    ly.wait()
    kept = {("x", 0): ax[:3], ("d", 0): ad[:3]}

    def keep(name, value):
        kept[name] = value

    half_x = pl.multiple_of(320 * rep, 64)
    far_x = pl.multiple_of(320 * (1 - rep), 64)
    half_h = pl.multiple_of(432 * rep, 16)
    far_h = pl.multiple_of(432 * (1 - rep), 16)

    def do_gate_up(c):
        kept["c", c, 0], kept["c", c, 1] = gate_up(c)

    def do_activate(c):
        arrived(kept.pop(("d", c, 0)) + kept.pop(("d", c, 1)))
        copies, saved = activate(c)
        keep(("e", c, 0), copies)
        keep(("saved", c), saved)

    def do_derive(c):
        arrived(kept.pop(("d", c, 2)))
        keep(("e", c, 1), derive(c, kept.pop(("saved", c))))

    def do_project(c):
        arrived(kept.pop(("f", c, 0)))
        keep(("g", 0, c), project(c))

    def do_pull_back(c):
        arrived(kept.pop(("f", c, 1)))
        keep(("pg", c), send(full.at[c, pl.ds(1, 2)], far.at[c], p_s.at[3 + c], p_r.at[3 + c], pdev))
        keep(("g", 1, c), pull_back(c))

    def turn_tokens():
        for j in range(5):
            xt[pl.ds(128 * j, 128), :] = xf[:, pl.ds(128 * j, 128)].T
        keep("px", send(xt.at[pl.ds(far_x, 320)], xt_far, p_s.at[1], p_r.at[1], pdev))

    def turn_hidden():
        for j in range(7):
            lanes = pl.ds(128 * j, 128)
            block = [full[c, 0, :, :, lanes].reshape(C, 128) for c in range(2)]
            ht[pl.ds(128 * j, 128), :] = jnp.concatenate(block, axis=0).T
        keep("ph", send(ht.at[pl.ds(far_h, 432)], ht_far, p_s.at[2], p_r.at[2], pdev))

    steps = {
        "fx": lambda: keep(("x", 1), spread_on(xf, 0, ax)),
        "fd": lambda: keep(("d", 1), spread_on(df, 1, ad)),
        "dy": lambda: keep("py", send(df, dy_far, p_s.at[0], p_r.at[0], pdev)),
        "xt": turn_tokens,
        "ht": turn_hidden,
        "r01": lambda: keep(("g", 0), reduce_on(0, kept.pop(("g", 0, 1)))),
        "r11": lambda: keep(("g", 1), reduce_on(1, kept.pop(("g", 1, 1)))),
    }
    for c in range(2):
        steps[f"gu{c}"] = lambda c=c: do_gate_up(c)
        steps[f"bk{c}"] = lambda c=c: keep(("c", c, 2), back_part(c))
        steps[f"act{c}"] = lambda c=c: do_activate(c)
        steps[f"der{c}"] = lambda c=c: do_derive(c)
        steps[f"pr{c}"] = lambda c=c: do_project(c)
        steps[f"pb{c}"] = lambda c=c: do_pull_back(c)
        for g in range(3):
            steps[f"s{c}{g}"] = lambda c=c, g=g: keep(("d", c, g), scatter_on(c, g, kept.pop(("c", c, g))))
        for g in range(2):
            steps[f"f{c}{g}"] = lambda c=c, g=g: keep(("f", c, g), gather_on(c, g, kept.pop(("e", c, g))))
    def token_terms():
        arrived([kept["px"], kept["py"]])
        for ref, at in ((xt.at[pl.ds(half_x, 320)], 0), (xt_far, ROWS)):
            hi, lo = split(ref[...])
            xth[pl.ds(0, 320), pl.ds(at, ROWS)] = hi
            xth[pl.ds(320, 320), pl.ds(at, ROWS)] = lo
        for c in range(2):
            dh[pl.ds(C * c, C), :] = ds_[c, pl.ds(0, C), :]
            dl[pl.ds(C * c, C), :] = ds_[c, pl.ds(C, C), :]
        dh[pl.ds(ROWS, ROWS), :], dl[pl.ds(ROWS, ROWS), :] = split(dy_far[...])

    def down_gradient():
        arrived([kept["ph"]])
        for ref, at in ((ht.at[pl.ds(half_h, 432)], 0), (ht_far, ROWS)):
            hi, lo = split(ref[...])
            hth[pl.ds(0, 432), pl.ds(at, ROWS)] = hi
            hth[pl.ds(432, 432), pl.ds(at, ROWS)] = lo
        gd_o[...] = dot3(hth[...], dh[...], dl[...], NN)

    def gate_up_gradients():
        arrived([kept["pg", 0], kept["pg", 1]])
        for i, o in enumerate((gg_o, gu_o)):
            for c in range(2):
                at = pl.ds(ROWS + C * c, C)
                bh[i, at, :], bl[i, at, :] = split(far[c, i].reshape(C, HP))
            o[...] = dot3(xth[...], bh[i], bl[i], NN)[:, :H]

    steps["tt"] = token_terms
    steps["gd"] = down_gradient
    steps["gw"] = gate_up_gradients
    for name in ORDER:
        steps[name]()

    arrived(kept["g", 0, 0] + kept["g", 0])
    out_o[...] = ring_sum(0, 0) + rx[0]
    arrived(kept["g", 1, 0])
    near = ring_sum(1, 0)
    if FAR_DIRECT:
        arrived(kept["g", 1, 1])
        gtok_o[...] = near + rf[0] + rf[1] + rf[2] + rf[3]
    else:
        arrived(kept["g", 1])
        gtok_o[...] = near + rx[1]
    for c in sent:
        c.wait_send()


def write(*refs):
    copies = []
    for i in range(5):
        src, dst, sems = refs[i], refs[5 + i], refs[10]
        n = PIECES[i]
        rows = src.shape[0] // n
        for k in range(n):
            at = pl.ds(rows * k, rows)
            copies.append(pltpu.make_async_copy(src.at[at], dst.at[at], sems.at[i, k]))
    for c in copies:
        c.start()
    for c in copies:
        c.wait()


def shards(tokens, cotangent, w_gate, w_up, w_down):
    v = pltpu.VMEM
    dma = pltpu.SemaphoreType.DMA
    cy = HP - CX
    scratch = [
        v((ROWS, W), F32), v((ROWS, W), F32), v((2, 2 * C, W), BF16), v((2, 2 * C, W), BF16),
        *[v((HP, W), F32)] * 3, *[v((HP, W), BF16)] * 6, *[v((W, HP), BF16)] * 6,
        v((2, 3, 2, 32, HP), F32), v((2, 3, 32, CX), F32), v((2, 3, 3, 8, CX), F32),
        v((2, 3, 3, 2, 8, cy), F32), v((2, 3, 8, cy), F32), v((2, 3, 32, CX), F32),
        v((2, 3, 2, 8, cy), F32), v((2, 3, 2, 32, HP), F32),
        v((W, ROWS), F32), v((320, ROWS), F32), v((ROWS, W), F32), v((HP, ROWS), F32), v((432, ROWS), F32),
        v((2, 2, 2, 32, HP), F32),
        v((640, 256), BF16), v((864, 256), BF16),
        v((2, 256, HP), BF16), v((2, 256, HP), BF16), v((256, W), BF16), v((256, W), BF16),
        v((2, 2, C, W), F32), v((2, 2, 3, 16, W), F32), v((2, 16, W), F32), v((2, 16, W), F32), v((4, 16, W), F32),
        dma((2, 7)), dma((2, 7)), dma((2, 3, 8)), dma((2, 3, 8)), dma((2, 2, 8)), dma((2, 2, 8)),
        dma((2, 2, 2, 4)), dma((2, 2, 2, 4)), dma((5,)), dma((5,)), dma((5,)),
    ]
    any_ = pl.BlockSpec(memory_space=pl.ANY)
    vmem = pl.BlockSpec(memory_space=pltpu.VMEM)
    hbm = pl.BlockSpec(memory_space=pltpu.HBM)
    shapes = [(16, W), (16, W), (320, H), (320, H), (432, W)]
    results = pl.pallas_call(
        kernel,
        out_shape=[v(s, F32) for s in shapes],
        in_specs=[hbm] * 5,
        out_specs=[vmem] * 5,
        scratch_shapes=scratch,
        compiler_params=pltpu.CompilerParams(
            collective_id=0, has_side_effects=True, vmem_limit_bytes=48 << 20
        ),
    )(*[pltpu.with_memory_space_constraint(a, pltpu.HBM) for a in (tokens, cotangent, w_gate.T, w_up.T, w_down)])
    results = [pltpu.with_memory_space_constraint(r, pltpu.VMEM) for r in results]
    out, gtok, gg, gu, gd = pl.pallas_call(
        write,
        out_shape=[jax.ShapeDtypeStruct(s, F32) for s in shapes],
        in_specs=[vmem] * 5,
        out_specs=[any_] * 5,
        scratch_shapes=[dma((5, max(PIECES)))],
    )(*results)
    return out, gtok, gg[None, None], gu[None, None], gd[None, None]


def solution(mesh):
    return jax.shard_map(
        shards,
        mesh=mesh,
        in_specs=(
            P(("rep", "hid"), "width"), P(("rep", "hid"), "width"),
            P("width", "hid"), P("width", "hid"), P("hid", "width"),
        ),
        out_specs=(
            P(("rep", "hid"), "width"), P(("rep", "hid"), "width"),
            P("width", "rep", None, "hid"), P("width", "rep", None, "hid"),
            P("hid", "rep", None, "width"),
        ),
        check_vma=False,
    )
```

```python
import functools

import jax
import jax.numpy as jnp
from jax import lax
from jax.experimental import pallas as pl
from jax.experimental.pallas import tpu as pltpu
from jax.sharding import PartitionSpec as P

MESH = pl.DeviceIdType.MESH
F32 = jnp.float32
BF16 = jnp.bfloat16
NN = (((1,), (0,)), ((), ()))
ROWS = 128
W = 640
H = 864
HP = 896
C = 64
CX = 512
EX = (512, 384)
SX, SY = pl.ds(0, CX), pl.ds(CX, HP - CX)
LANES = (SX, SY)
SIDES = (0, 1)
GX = [pl.ds(0, e) for e in EX]
GY = [pl.ds(e, HP - e) for e in EX]
GROUPS = ((0, 1), (1, 1), (2, 1))
COLUMNS = (pl.ds(0, 640),)
FAR_DIRECT = True
GROUPS_BACK = ((0, 1), (1, 2))
PIECES = (1, 1, 1, 1, 1)
ORDER = (
    "fx", "gu0", "fd", "bk0", "gu1", "x00", "y00", "x01", "y01", "bk1", "x02", "y02", "x10", "x11", "x12", "y10", "y11", "y12",
    "act0", "dy", "der0", "act1", "der1", "f00", "f10", "f11", "f01", "pr0", "xt", "pr1", "ht", "tt", "pb1", "gd", "pb0", "r01", "gw",
)


def split(v):
    hi = v.astype(BF16)
    return hi, (v - hi.astype(F32)).astype(BF16)


def dot(a, b, dims):
    return lax.dot_general(a, b, dims, preferred_element_type=F32)


def dot3(stack, b_hi, b_lo, dims):
    m = stack.shape[0] // 2
    both = dot(stack, b_hi, dims)
    return both[:m] + both[m:] + dot(stack[:m], b_lo, dims)


def kernel(
    tok_in, cot_in, wg_in, wu_in, wd_in,
    out_o, gtok_o, gg_o, gu_o, gd_o,
    xf, df, xs, ds_, wgf, wuf, wdf, wgh, wgl, wuh, wul, wdh, wdl,
    wgth, wgtl, wuth, wutl, wdth, wdtl,
    part, r1, r2, r3, r4, s1, s3, full,
    xt, xt_far, dy_far, ht, ht_far, far,
    xth, hth, bh, bl, dh, dl,
    op, rz, sz, rx, rf,
    a_s, a_r, c_s, c_r, e_s, e_r, g_s, g_r, p_s, p_r, l_s,
):
    rep = lax.axis_index("rep")
    w = lax.axis_index("width")
    h = lax.axis_index("hid")
    y, xl = w // 2, w % 2
    z, xh = h // 2, h % 2

    def ydev(k):
        return (rep, ((y + k) % 4) * 2 + xl, h)

    xdev = (rep, y * 2 + (1 - xl), h)

    def zdev(k):
        return (rep, w, ((z + k) % 4) * 2 + xh)

    def odev(k):
        return (rep, w, ((z + k) % 4) * 2 + (1 - xh))

    hdev = odev(0)
    pdev = (1 - rep, w, h)
    sent = []

    def send(src, dst, s, r, device):
        c = pltpu.make_async_remote_copy(
            src_ref=src, dst_ref=dst, send_sem=s, recv_sem=r,
            device_id=device, device_id_type=MESH,
        )
        c.start()
        sent.append(c)
        return c

    def local(src, dst, i):
        c = pltpu.make_async_copy(src, dst, l_s.at[i])
        c.start()
        return c

    def row8(k):
        return pl.ds(pl.multiple_of(8 * k, 8), 8)

    def arrived(copies):
        for d in copies:
            d.wait_recv()

    def ring(c, k=0):
        return pl.ds(pl.multiple_of(C * c + 16 * ((z + k) % 4), 16), 16)

    lx = local(tok_in, xf.at[ring(0)], 0)
    ly = local(cot_in, df.at[ring(0)], 1)
    lg = local(wg_in, wgf.at[pl.ds(0, H)], 2)
    lu = local(wu_in, wuf.at[pl.ds(0, H)], 3)
    ld = local(wd_in, wdf.at[pl.ds(0, H)], 4)
    for ref in (wgf, wuf, wdf):
        ref[pl.ds(H, HP - H), :] = jnp.zeros((HP - H, W), F32)

    barrier = pltpu.get_barrier_semaphore()
    peers = [ydev(k) for k in (2, 1, 3)] + [xdev] + [zdev(k) for k in (2, 1, 3)] + [hdev] + [pdev]
    for d in peers:
        pl.semaphore_signal(barrier, inc=1, device_id=d, device_id_type=MESH)
    pl.semaphore_wait(barrier, len(peers))

    def spread(src, dst, i):
        out = [send(src, dst.at[ring(0)], a_s.at[i, k], a_r.at[i, k], zdev(k)) for k in (2, 1, 3)]
        out.append(send(src, dst.at[ring(1)], a_s.at[i, 0], a_r.at[i, 0], hdev))
        return out

    def spread_on(dst, i, first):
        arrived(first[3:])
        block = dst.at[ring(1)]
        return [send(block, block, a_s.at[i, 3 + k], a_r.at[i, 3 + k], zdev(k)) for k in (2, 1, 3)]

    ax = spread(tok_in, xf, 0)
    ad = spread(cot_in, df, 1)

    def halves(src, hi_ref, lo_ref, turned_hi, turned_lo):
        def body(i, _):
            at = pl.ds(pl.multiple_of(i * 128, 128), 128)
            v = src[at, :]
            hi_ref[at, :], lo_ref[at, :] = split(v)
            turned_hi[:, at], turned_lo[:, at] = split(v.T)
            return 0

        lax.fori_loop(0, HP // 128, body, 0)

    def stacked(src, dst, c):
        hi, lo = split(src[pl.ds(C * c, C), :])
        dst[c, pl.ds(0, C), :] = hi
        dst[c, pl.ds(C, C), :] = lo

    def halved(v):
        return v.reshape(2, C // 2, v.shape[1])

    def scatter(c, g):
        lo, n = GROUPS[g]
        arrays = pl.ds(lo, n)
        out = [
            send(
                part.at[c, arrays, 1 - xl, :, SX], r1.at[c, arrays],
                c_s.at[c, g, 0], c_r.at[c, g, 0], xdev,
            )
        ]
        for k in (2, 1, 3):
            out.append(
                send(
                    part.at[c, arrays, :, row8((y + k) % 4), SY], r3.at[c, k - 1, arrays],
                    c_s.at[c, g, k], c_r.at[c, g, k], ydev(k),
                )
            )
        return out

    def scatter_x(c, g, first):
        lo, n = GROUPS[g]
        arrays = pl.ds(lo, n)
        arrived(first[:1])
        for a in range(lo, lo + n):
            s1[c, a] = part[c, a, xl, :, SX] + r1[c, a]
        out = []
        for k in (2, 1, 3):
            out.append(
                send(
                    s1.at[c, arrays, row8((y + k) % 4)], r2.at[c, k - 1, arrays],
                    c_s.at[c, g, 3 + k], c_r.at[c, g, 3 + k], ydev(k),
                )
            )
        return out

    def scatter_y(c, g, first):
        lo, n = GROUPS[g]
        arrays = pl.ds(lo, n)
        arrived(first[1:])
        for a in range(lo, lo + n):
            s3[c, a] = part[c, a, :, row8(y), SY] + r3[c, 0, a] + r3[c, 1, a] + r3[c, 2, a]
        return [
            send(
                s3.at[c, arrays, 1 - xl], r4.at[c, arrays],
                c_s.at[c, g, 7], c_r.at[c, g, 7], xdev,
            )
        ]

    def summed(c, a, side):
        if side == 0:
            return s1[c, a, row8(y), :] + r2[c, 0, a] + r2[c, 1, a] + r2[c, 2, a]
        return s3[c, a, xl] + r4[c, a]

    def gather(c, g, side):
        lo, n = GROUPS_BACK[g]
        arrays = pl.ds(lo, n)
        if side == 1:
            mine = full.at[c, arrays, xl, row8(y), GY[g]]
            return [send(mine, mine, e_s.at[c, g, 0], e_r.at[c, g, 0], xdev)]
        mine = full.at[c, arrays, xl, row8(y), GX[g]]
        return [send(mine, mine, e_s.at[c, g, k], e_r.at[c, g, k], ydev(k)) for k in (2, 1, 3)]

    def gather_on(c, g, first):
        lo, n = GROUPS_BACK[g]
        arrays = pl.ds(lo, n)
        out = []
        arrived(first[:1])
        pair = full.at[c, arrays, :, row8(y), GY[g]]
        for k in (2, 1, 3):
            out.append(send(pair, pair, e_s.at[c, g, 3 + k], e_r.at[c, g, 3 + k], ydev(k)))
        arrived(first[1:])
        half = full.at[c, arrays, xl, :, GX[g]]
        out.append(send(half, half, e_s.at[c, g, 7], e_r.at[c, g, 7], xdev))
        return out

    def activate(c, side):
        gate = summed(c, 0, side)
        up = summed(c, 1, side)
        logistic = 1.0 / (1.0 + jnp.exp(-gate))
        full[c, 0, xl, row8(y), LANES[side]] = gate * logistic * up
        return gate, up, logistic

    def derive(c, side, gate, up, logistic):
        back = summed(c, 2, side)
        full[c, 1, xl, row8(y), LANES[side]] = back * up * logistic * (1.0 + gate * (1.0 - logistic))
        full[c, 2, xl, row8(y), LANES[side]] = back * gate * logistic

    def whole(c, a):
        return full[c, a].reshape(C, HP)

    def reduce_rows(i, c, cols, part_no):
        return [
            send(
                op.at[i, c, ring(0, k), cols], rz.at[i, c, k - 1, :, cols],
                g_s.at[i, c, part_no, k], g_r.at[i, c, part_no, k], zdev(k),
            )
            for k in (2, 1, 3)
        ]

    def ring_sum(i, c):
        return op[i, c, ring(0), :] + rz[i, c, 0] + rz[i, c, 1] + rz[i, c, 2]

    def reduce_far(i, cols, part_no):
        return [
            send(
                op.at[i, 1, ring(0, k), cols], rf.at[k, :, cols],
                g_s.at[i, 1, part_no, k], g_r.at[i, 1, part_no, k], odev(k),
            )
            for k in (0, 2, 1, 3)
        ]

    def reduce_on(i, first):
        arrived(first)
        sz[i] = ring_sum(i, 1)
        return [send(sz.at[i], rx.at[i], g_s.at[i, 0, 0, 0], g_r.at[i, 0, 0, 0], hdev)]

    def project(c):
        hi, lo = split(whole(c, 0))
        op[0, c] = dot3(jnp.concatenate([hi, lo], axis=0), wdh[...], wdl[...], NN)
        return reduce_rows(0, c, pl.ds(0, W), 0)

    def pull_back(c):
        terms = []
        for i in range(2):
            at = pl.ds(C * c, C)
            hi, lo = split(whole(c, 1 + i))
            bh[i, at, :], bl[i, at, :] = hi, lo
            terms.append(jnp.concatenate([hi, lo], axis=0))
        copies = []
        for part_no, cols in enumerate(COLUMNS):
            op[1, c, :, cols] = dot3(terms[0], wgh[:, cols], wgl[:, cols], NN) + dot3(terms[1], wuh[:, cols], wul[:, cols], NN)
            if c == 1 and FAR_DIRECT:
                copies += reduce_far(1, cols, part_no)
            else:
                copies += reduce_rows(1, c, cols, part_no)
        return copies

    def gate_up(c):
        arrived(kept.pop(("x", c)))
        stacked(xf, xs, c)
        part[c, 0] = halved(dot3(xs[c], wgth[...], wgtl[...], NN))
        gate = scatter(c, 0)
        part[c, 1] = halved(dot3(xs[c], wuth[...], wutl[...], NN))
        return gate, scatter(c, 1)

    def back_part(c):
        arrived(kept.pop(("d", c)))
        stacked(df, ds_, c)
        part[c, 2] = halved(dot3(ds_[c], wdth[...], wdtl[...], NN))
        return scatter(c, 2)

    lg.wait()
    halves(wgf, wgh, wgl, wgth, wgtl)
    lu.wait()
    halves(wuf, wuh, wul, wuth, wutl)
    ld.wait()
    halves(wdf, wdh, wdl, wdth, wdtl)
    lx.wait()
    ly.wait()
    kept = {("x", 0): ax[:3], ("d", 0): ad[:3]}

    def keep(name, value):
        kept[name] = value

    half_x = pl.multiple_of(320 * rep, 64)
    far_x = pl.multiple_of(320 * (1 - rep), 64)
    half_h = pl.multiple_of(432 * rep, 16)
    far_h = pl.multiple_of(432 * (1 - rep), 16)

    def do_gate_up(c):
        kept["c", c, 0], kept["c", c, 1] = gate_up(c)

    def by_side(copies, side):
        return copies[:3] if side == 0 else copies[3:]

    def do_activate(c):
        copies = [None, None]
        gate, up = kept.pop(("d", c, 0)), kept.pop(("d", c, 1))
        for side in SIDES:
            arrived(by_side(gate, side) + by_side(up, side))
            keep(("saved", c, side), activate(c, side))
            copies[side] = gather(c, 0, side)
        keep(("e", c, 0), copies[1] + copies[0])

    def do_derive(c):
        copies = [None, None]
        back = kept.pop(("d", c, 2))
        for side in (0, 1):
            arrived(by_side(back, side))
            derive(c, side, *kept.pop(("saved", c, side)))
            copies[side] = gather(c, 1, side)
        keep(("e", c, 1), copies[1] + copies[0])

    def do_project(c):
        arrived(kept.pop(("f", c, 0)))
        keep(("g", 0, c), project(c))

    def do_pull_back(c):
        arrived(kept.pop(("f", c, 1)))
        keep(("pg", c), send(full.at[c, pl.ds(1, 2)], far.at[c], p_s.at[3 + c], p_r.at[3 + c], pdev))
        keep(("g", 1, c), pull_back(c))

    def turn_tokens():
        for j in range(5):
            xt[pl.ds(128 * j, 128), :] = xf[:, pl.ds(128 * j, 128)].T
        keep("px", send(xt.at[pl.ds(far_x, 320)], xt_far, p_s.at[1], p_r.at[1], pdev))

    def turn_hidden():
        for j in range(7):
            lanes = pl.ds(128 * j, 128)
            block = [full[c, 0, :, :, lanes].reshape(C, 128) for c in range(2)]
            ht[pl.ds(128 * j, 128), :] = jnp.concatenate(block, axis=0).T
        keep("ph", send(ht.at[pl.ds(far_h, 432)], ht_far, p_s.at[2], p_r.at[2], pdev))

    steps = {
        "fx": lambda: keep(("x", 1), spread_on(xf, 0, ax)),
        "fd": lambda: keep(("d", 1), spread_on(df, 1, ad)),
        "dy": lambda: keep("py", send(df, dy_far, p_s.at[0], p_r.at[0], pdev)),
        "xt": turn_tokens,
        "ht": turn_hidden,
        "r01": lambda: keep(("g", 0), reduce_on(0, kept.pop(("g", 0, 1)))),
        "r11": lambda: keep(("g", 1), reduce_on(1, kept.pop(("g", 1, 1)))),
    }
    for c in range(2):
        steps[f"gu{c}"] = lambda c=c: do_gate_up(c)
        steps[f"bk{c}"] = lambda c=c: keep(("c", c, 2), back_part(c))
        steps[f"act{c}"] = lambda c=c: do_activate(c)
        steps[f"der{c}"] = lambda c=c: do_derive(c)
        steps[f"pr{c}"] = lambda c=c: do_project(c)
        steps[f"pb{c}"] = lambda c=c: do_pull_back(c)
        for g in range(3):
            steps[f"x{c}{g}"] = lambda c=c, g=g: keep(("dx", c, g), scatter_x(c, g, kept["c", c, g]))
            steps[f"y{c}{g}"] = lambda c=c, g=g: keep(
                ("d", c, g), kept.pop(("dx", c, g)) + scatter_y(c, g, kept.pop(("c", c, g)))
            )
        for g in range(2):
            steps[f"f{c}{g}"] = lambda c=c, g=g: keep(("f", c, g), gather_on(c, g, kept.pop(("e", c, g))))
    def token_terms():
        arrived([kept["px"], kept["py"]])
        for ref, at in ((xt.at[pl.ds(half_x, 320)], 0), (xt_far, ROWS)):
            hi, lo = split(ref[...])
            xth[pl.ds(0, 320), pl.ds(at, ROWS)] = hi
            xth[pl.ds(320, 320), pl.ds(at, ROWS)] = lo
        for c in range(2):
            dh[pl.ds(C * c, C), :] = ds_[c, pl.ds(0, C), :]
            dl[pl.ds(C * c, C), :] = ds_[c, pl.ds(C, C), :]
        dh[pl.ds(ROWS, ROWS), :], dl[pl.ds(ROWS, ROWS), :] = split(dy_far[...])

    def down_gradient():
        arrived([kept["ph"]])
        for ref, at in ((ht.at[pl.ds(half_h, 432)], 0), (ht_far, ROWS)):
            hi, lo = split(ref[...])
            hth[pl.ds(0, 432), pl.ds(at, ROWS)] = hi
            hth[pl.ds(432, 432), pl.ds(at, ROWS)] = lo
        gd_o[...] = dot3(hth[...], dh[...], dl[...], NN)

    def gate_up_gradients():
        arrived([kept["pg", 0], kept["pg", 1]])
        for i, o in enumerate((gg_o, gu_o)):
            for c in range(2):
                at = pl.ds(ROWS + C * c, C)
                bh[i, at, :], bl[i, at, :] = split(far[c, i].reshape(C, HP))
            o[...] = dot3(xth[...], bh[i], bl[i], NN)[:, :H]

    steps["tt"] = token_terms
    steps["gd"] = down_gradient
    steps["gw"] = gate_up_gradients
    for name in ORDER:
        steps[name]()

    arrived(kept["g", 0, 0] + kept["g", 0])
    out_o[...] = ring_sum(0, 0) + rx[0]
    arrived(kept["g", 1, 0])
    near = ring_sum(1, 0)
    if FAR_DIRECT:
        arrived(kept["g", 1, 1])
        gtok_o[...] = near + rf[0] + rf[1] + rf[2] + rf[3]
    else:
        arrived(kept["g", 1])
        gtok_o[...] = near + rx[1]
    for c in sent:
        c.wait_send()


def write(*refs):
    copies = []
    for i in range(5):
        src, dst, sems = refs[i], refs[5 + i], refs[10]
        n = PIECES[i]
        rows = src.shape[0] // n
        for k in range(n):
            at = pl.ds(rows * k, rows)
            copies.append(pltpu.make_async_copy(src.at[at], dst.at[at], sems.at[i, k]))
    for c in copies:
        c.start()
    for c in copies:
        c.wait()


def shards(tokens, cotangent, w_gate, w_up, w_down):
    v = pltpu.VMEM
    dma = pltpu.SemaphoreType.DMA
    cy = HP - CX
    scratch = [
        v((ROWS, W), F32), v((ROWS, W), F32), v((2, 2 * C, W), BF16), v((2, 2 * C, W), BF16),
        *[v((HP, W), F32)] * 3, *[v((HP, W), BF16)] * 6, *[v((W, HP), BF16)] * 6,
        v((2, 3, 2, 32, HP), F32), v((2, 3, 32, CX), F32), v((2, 3, 3, 8, CX), F32),
        v((2, 3, 3, 2, 8, cy), F32), v((2, 3, 8, cy), F32), v((2, 3, 32, CX), F32),
        v((2, 3, 2, 8, cy), F32), v((2, 3, 2, 32, HP), F32),
        v((W, ROWS), F32), v((320, ROWS), F32), v((ROWS, W), F32), v((HP, ROWS), F32), v((432, ROWS), F32),
        v((2, 2, 2, 32, HP), F32),
        v((640, 256), BF16), v((864, 256), BF16),
        v((2, 256, HP), BF16), v((2, 256, HP), BF16), v((256, W), BF16), v((256, W), BF16),
        v((2, 2, C, W), F32), v((2, 2, 3, 16, W), F32), v((2, 16, W), F32), v((2, 16, W), F32), v((4, 16, W), F32),
        dma((2, 7)), dma((2, 7)), dma((2, 3, 8)), dma((2, 3, 8)), dma((2, 2, 8)), dma((2, 2, 8)),
        dma((2, 2, 2, 4)), dma((2, 2, 2, 4)), dma((5,)), dma((5,)), dma((5,)),
    ]
    any_ = pl.BlockSpec(memory_space=pl.ANY)
    vmem = pl.BlockSpec(memory_space=pltpu.VMEM)
    hbm = pl.BlockSpec(memory_space=pltpu.HBM)
    shapes = [(16, W), (16, W), (320, H), (320, H), (432, W)]
    results = pl.pallas_call(
        kernel,
        out_shape=[v(s, F32) for s in shapes],
        in_specs=[hbm] * 5,
        out_specs=[vmem] * 5,
        scratch_shapes=scratch,
        compiler_params=pltpu.CompilerParams(
            collective_id=0, has_side_effects=True, vmem_limit_bytes=48 << 20
        ),
    )(*[pltpu.with_memory_space_constraint(a, pltpu.HBM) for a in (tokens, cotangent, w_gate.T, w_up.T, w_down)])
    results = [pltpu.with_memory_space_constraint(r, pltpu.VMEM) for r in results]
    out, gtok, gg, gu, gd = pl.pallas_call(
        write,
        out_shape=[jax.ShapeDtypeStruct(s, F32) for s in shapes],
        in_specs=[vmem] * 5,
        out_specs=[any_] * 5,
        scratch_shapes=[dma((5, max(PIECES)))],
    )(*results)
    return out, gtok, gg[None, None], gu[None, None], gd[None, None]


def solution(mesh):
    return jax.shard_map(
        shards,
        mesh=mesh,
        in_specs=(
            P(("rep", "hid"), "width"), P(("rep", "hid"), "width"),
            P("width", "hid"), P("width", "hid"), P("hid", "width"),
        ),
        out_specs=(
            P(("rep", "hid"), "width"), P(("rep", "hid"), "width"),
            P("width", "rep", None, "hid"), P("width", "rep", None, "hid"),
            P("hid", "rep", None, "width"),
        ),
        check_vma=False,
    )
```

```python
import functools

import jax
import jax.numpy as jnp
from jax import lax
from jax.experimental import pallas as pl
from jax.experimental.pallas import tpu as pltpu
from jax.sharding import PartitionSpec as P

MESH = pl.DeviceIdType.MESH
F32 = jnp.float32
BF16 = jnp.bfloat16
NN = (((1,), (0,)), ((), ()))
ROWS = 128
W = 640
H = 864
HP = 896
C = 64
CX = 512
EX = ((512, 512), (512, 384))
SX, SY = pl.ds(0, CX), pl.ds(CX, HP - CX)
LANES = (SX, SY)
SIDES = (0, 1)
GX = [[pl.ds(0, e) for e in row] for row in EX]
GY = [[pl.ds(e, HP - e) for e in row] for row in EX]
GROUPS = ((0, 1), (1, 1), (2, 1))
COLUMNS = (pl.ds(0, 640),)
FAR_DIRECT = True
GROUPS_BACK = ((0, 1), (1, 2))
PIECES = (1, 1, 1, 1, 1)
ORDER = (
    "fx", "gu0", "fd", "bk0", "gu1", "x00", "y00", "x01", "y01", "bk1", "x02", "y02", "x10", "x11", "x12", "y10", "y11", "y12",
    "act0", "dy", "der0", "act1", "der1", "f00", "f10", "f11", "f01", "pr0", "xt", "pr1", "ht", "tt", "pb1", "gd", "pb0", "r01", "gw",
)


def split(v):
    hi = v.astype(BF16)
    return hi, (v - hi.astype(F32)).astype(BF16)


def dot(a, b, dims):
    return lax.dot_general(a, b, dims, preferred_element_type=F32)


def dot3(stack, b_hi, b_lo, dims):
    m = stack.shape[0] // 2
    both = dot(stack, b_hi, dims)
    return both[:m] + both[m:] + dot(stack[:m], b_lo, dims)


def kernel(
    tok_in, cot_in, wg_in, wu_in, wd_in,
    out_o, gtok_o, gg_o, gu_o, gd_o,
    xf, df, xs, ds_, wgf, wuf, wdf, wgh, wgl, wuh, wul, wdh, wdl,
    wgth, wgtl, wuth, wutl, wdth, wdtl,
    part, r1, r2, r3, r4, s1, s3, full,
    xt, xt_far, dy_far, ht, ht_far, far,
    xth, hth, bh, bl, dh, dl,
    op, rz, sz, rx, rf,
    a_s, a_r, c_s, c_r, e_s, e_r, g_s, g_r, p_s, p_r, l_s,
):
    rep = lax.axis_index("rep")
    w = lax.axis_index("width")
    h = lax.axis_index("hid")
    y, xl = w // 2, w % 2
    z, xh = h // 2, h % 2

    def ydev(k):
        return (rep, ((y + k) % 4) * 2 + xl, h)

    xdev = (rep, y * 2 + (1 - xl), h)

    def zdev(k):
        return (rep, w, ((z + k) % 4) * 2 + xh)

    def odev(k):
        return (rep, w, ((z + k) % 4) * 2 + (1 - xh))

    hdev = odev(0)
    pdev = (1 - rep, w, h)
    sent = []

    def send(src, dst, s, r, device):
        c = pltpu.make_async_remote_copy(
            src_ref=src, dst_ref=dst, send_sem=s, recv_sem=r,
            device_id=device, device_id_type=MESH,
        )
        c.start()
        sent.append(c)
        return c

    def local(src, dst, i):
        c = pltpu.make_async_copy(src, dst, l_s.at[i])
        c.start()
        return c

    def row8(k):
        return pl.ds(pl.multiple_of(8 * k, 8), 8)

    def arrived(copies):
        for d in copies:
            d.wait_recv()

    def ring(c, k=0):
        return pl.ds(pl.multiple_of(C * c + 16 * ((z + k) % 4), 16), 16)

    lx = local(tok_in, xf.at[ring(0)], 0)
    ly = local(cot_in, df.at[ring(0)], 1)
    lg = local(wg_in, wgf.at[pl.ds(0, H)], 2)
    lu = local(wu_in, wuf.at[pl.ds(0, H)], 3)
    ld = local(wd_in, wdf.at[pl.ds(0, H)], 4)
    for ref in (wgf, wuf, wdf):
        ref[pl.ds(H, HP - H), :] = jnp.zeros((HP - H, W), F32)

    barrier = pltpu.get_barrier_semaphore()
    peers = [ydev(k) for k in (2, 1, 3)] + [xdev] + [zdev(k) for k in (2, 1, 3)] + [hdev] + [pdev]
    for d in peers:
        pl.semaphore_signal(barrier, inc=1, device_id=d, device_id_type=MESH)
    pl.semaphore_wait(barrier, len(peers))

    def spread(src, dst, i):
        out = [send(src, dst.at[ring(0)], a_s.at[i, k], a_r.at[i, k], zdev(k)) for k in (2, 1, 3)]
        out.append(send(src, dst.at[ring(1)], a_s.at[i, 0], a_r.at[i, 0], hdev))
        return out

    def spread_on(dst, i, first):
        arrived(first[3:])
        block = dst.at[ring(1)]
        return [send(block, block, a_s.at[i, 3 + k], a_r.at[i, 3 + k], zdev(k)) for k in (2, 1, 3)]

    ax = spread(tok_in, xf, 0)
    ad = spread(cot_in, df, 1)

    def halves(src, hi_ref, lo_ref, turned_hi, turned_lo):
        def body(i, _):
            at = pl.ds(pl.multiple_of(i * 128, 128), 128)
            v = src[at, :]
            hi_ref[at, :], lo_ref[at, :] = split(v)
            turned_hi[:, at], turned_lo[:, at] = split(v.T)
            return 0

        lax.fori_loop(0, HP // 128, body, 0)

    def stacked(src, dst, c):
        hi, lo = split(src[pl.ds(C * c, C), :])
        dst[c, pl.ds(0, C), :] = hi
        dst[c, pl.ds(C, C), :] = lo

    def halved(v):
        return v.reshape(2, C // 2, v.shape[1])

    def scatter(c, g):
        lo, n = GROUPS[g]
        arrays = pl.ds(lo, n)
        out = [
            send(
                part.at[c, arrays, 1 - xl, :, SX], r1.at[c, arrays],
                c_s.at[c, g, 0], c_r.at[c, g, 0], xdev,
            )
        ]
        for k in (2, 1, 3):
            out.append(
                send(
                    part.at[c, arrays, :, row8((y + k) % 4), SY], r3.at[c, k - 1, arrays],
                    c_s.at[c, g, k], c_r.at[c, g, k], ydev(k),
                )
            )
        return out

    def scatter_x(c, g, first):
        lo, n = GROUPS[g]
        arrays = pl.ds(lo, n)
        arrived(first[:1])
        for a in range(lo, lo + n):
            s1[c, a] = part[c, a, xl, :, SX] + r1[c, a]
        out = []
        for k in (2, 1, 3):
            out.append(
                send(
                    s1.at[c, arrays, row8((y + k) % 4)], r2.at[c, k - 1, arrays],
                    c_s.at[c, g, 3 + k], c_r.at[c, g, 3 + k], ydev(k),
                )
            )
        return out

    def scatter_y(c, g, first):
        lo, n = GROUPS[g]
        arrays = pl.ds(lo, n)
        arrived(first[1:])
        for a in range(lo, lo + n):
            s3[c, a] = part[c, a, :, row8(y), SY] + r3[c, 0, a] + r3[c, 1, a] + r3[c, 2, a]
        return [
            send(
                s3.at[c, arrays, 1 - xl], r4.at[c, arrays],
                c_s.at[c, g, 7], c_r.at[c, g, 7], xdev,
            )
        ]

    def summed(c, a, side):
        if side == 0:
            return s1[c, a, row8(y), :] + r2[c, 0, a] + r2[c, 1, a] + r2[c, 2, a]
        return s3[c, a, xl] + r4[c, a]

    def gather(c, g, side):
        lo, n = GROUPS_BACK[g]
        arrays = pl.ds(lo, n)
        if side == 1:
            mine = full.at[c, arrays, xl, row8(y), GY[c][g]]
            return [send(mine, mine, e_s.at[c, g, 0], e_r.at[c, g, 0], xdev)]
        mine = full.at[c, arrays, xl, row8(y), GX[c][g]]
        return [send(mine, mine, e_s.at[c, g, k], e_r.at[c, g, k], ydev(k)) for k in (2, 1, 3)]

    def gather_on(c, g, first):
        lo, n = GROUPS_BACK[g]
        arrays = pl.ds(lo, n)
        out = []
        arrived(first[:1])
        pair = full.at[c, arrays, :, row8(y), GY[c][g]]
        for k in (2, 1, 3):
            out.append(send(pair, pair, e_s.at[c, g, 3 + k], e_r.at[c, g, 3 + k], ydev(k)))
        arrived(first[1:])
        half = full.at[c, arrays, xl, :, GX[c][g]]
        out.append(send(half, half, e_s.at[c, g, 7], e_r.at[c, g, 7], xdev))
        return out

    def activate(c, side):
        gate = summed(c, 0, side)
        up = summed(c, 1, side)
        logistic = 1.0 / (1.0 + jnp.exp(-gate))
        full[c, 0, xl, row8(y), LANES[side]] = gate * logistic * up
        return gate, up, logistic

    def derive(c, side, gate, up, logistic):
        back = summed(c, 2, side)
        full[c, 1, xl, row8(y), LANES[side]] = back * up * logistic * (1.0 + gate * (1.0 - logistic))
        full[c, 2, xl, row8(y), LANES[side]] = back * gate * logistic

    def whole(c, a):
        return full[c, a].reshape(C, HP)

    def reduce_rows(i, c, cols, part_no):
        return [
            send(
                op.at[i, c, ring(0, k), cols], rz.at[i, c, k - 1, :, cols],
                g_s.at[i, c, part_no, k], g_r.at[i, c, part_no, k], zdev(k),
            )
            for k in (2, 1, 3)
        ]

    def ring_sum(i, c):
        return op[i, c, ring(0), :] + rz[i, c, 0] + rz[i, c, 1] + rz[i, c, 2]

    def reduce_far(i, cols, part_no):
        return [
            send(
                op.at[i, 1, ring(0, k), cols], rf.at[k, :, cols],
                g_s.at[i, 1, part_no, k], g_r.at[i, 1, part_no, k], odev(k),
            )
            for k in (0, 2, 1, 3)
        ]

    def reduce_on(i, first):
        arrived(first)
        sz[i] = ring_sum(i, 1)
        return [send(sz.at[i], rx.at[i], g_s.at[i, 0, 0, 0], g_r.at[i, 0, 0, 0], hdev)]

    def project(c):
        hi, lo = split(whole(c, 0))
        op[0, c] = dot3(jnp.concatenate([hi, lo], axis=0), wdh[...], wdl[...], NN)
        return reduce_rows(0, c, pl.ds(0, W), 0)

    def pull_back(c):
        terms = []
        for i in range(2):
            at = pl.ds(C * c, C)
            hi, lo = split(whole(c, 1 + i))
            bh[i, at, :], bl[i, at, :] = hi, lo
            terms.append(jnp.concatenate([hi, lo], axis=0))
        copies = []
        for part_no, cols in enumerate(COLUMNS):
            op[1, c, :, cols] = dot3(terms[0], wgh[:, cols], wgl[:, cols], NN) + dot3(terms[1], wuh[:, cols], wul[:, cols], NN)
            if c == 1 and FAR_DIRECT:
                copies += reduce_far(1, cols, part_no)
            else:
                copies += reduce_rows(1, c, cols, part_no)
        return copies

    def gate_up(c):
        arrived(kept.pop(("x", c)))
        stacked(xf, xs, c)
        part[c, 0] = halved(dot3(xs[c], wgth[...], wgtl[...], NN))
        gate = scatter(c, 0)
        part[c, 1] = halved(dot3(xs[c], wuth[...], wutl[...], NN))
        return gate, scatter(c, 1)

    def back_part(c):
        arrived(kept.pop(("d", c)))
        stacked(df, ds_, c)
        part[c, 2] = halved(dot3(ds_[c], wdth[...], wdtl[...], NN))
        return scatter(c, 2)

    lg.wait()
    halves(wgf, wgh, wgl, wgth, wgtl)
    lu.wait()
    halves(wuf, wuh, wul, wuth, wutl)
    ld.wait()
    halves(wdf, wdh, wdl, wdth, wdtl)
    lx.wait()
    ly.wait()
    kept = {("x", 0): ax[:3], ("d", 0): ad[:3]}

    def keep(name, value):
        kept[name] = value

    half_x = pl.multiple_of(320 * rep, 64)
    far_x = pl.multiple_of(320 * (1 - rep), 64)
    half_h = pl.multiple_of(432 * rep, 16)
    far_h = pl.multiple_of(432 * (1 - rep), 16)

    def do_gate_up(c):
        kept["c", c, 0], kept["c", c, 1] = gate_up(c)

    def by_side(copies, side):
        return copies[:3] if side == 0 else copies[3:]

    def do_activate(c):
        copies = [None, None]
        gate, up = kept.pop(("d", c, 0)), kept.pop(("d", c, 1))
        for side in SIDES:
            arrived(by_side(gate, side) + by_side(up, side))
            keep(("saved", c, side), activate(c, side))
            copies[side] = gather(c, 0, side)
        keep(("e", c, 0), copies[1] + copies[0])

    def do_derive(c):
        copies = [None, None]
        back = kept.pop(("d", c, 2))
        for side in (0, 1):
            arrived(by_side(back, side))
            derive(c, side, *kept.pop(("saved", c, side)))
            copies[side] = gather(c, 1, side)
        keep(("e", c, 1), copies[1] + copies[0])

    def do_project(c):
        arrived(kept.pop(("f", c, 0)))
        keep(("g", 0, c), project(c))

    def do_pull_back(c):
        arrived(kept.pop(("f", c, 1)))
        keep(("pg", c), send(full.at[c, pl.ds(1, 2)], far.at[c], p_s.at[3 + c], p_r.at[3 + c], pdev))
        keep(("g", 1, c), pull_back(c))

    def turn_tokens():
        for j in range(5):
            xt[pl.ds(128 * j, 128), :] = xf[:, pl.ds(128 * j, 128)].T
        keep("px", send(xt.at[pl.ds(far_x, 320)], xt_far, p_s.at[1], p_r.at[1], pdev))

    def turn_hidden():
        for j in range(7):
            lanes = pl.ds(128 * j, 128)
            block = [full[c, 0, :, :, lanes].reshape(C, 128) for c in range(2)]
            ht[pl.ds(128 * j, 128), :] = jnp.concatenate(block, axis=0).T
        keep("ph", send(ht.at[pl.ds(far_h, 432)], ht_far, p_s.at[2], p_r.at[2], pdev))

    steps = {
        "fx": lambda: keep(("x", 1), spread_on(xf, 0, ax)),
        "fd": lambda: keep(("d", 1), spread_on(df, 1, ad)),
        "dy": lambda: keep("py", send(df, dy_far, p_s.at[0], p_r.at[0], pdev)),
        "xt": turn_tokens,
        "ht": turn_hidden,
        "r01": lambda: keep(("g", 0), reduce_on(0, kept.pop(("g", 0, 1)))),
        "r11": lambda: keep(("g", 1), reduce_on(1, kept.pop(("g", 1, 1)))),
    }
    for c in range(2):
        steps[f"gu{c}"] = lambda c=c: do_gate_up(c)
        steps[f"bk{c}"] = lambda c=c: keep(("c", c, 2), back_part(c))
        steps[f"act{c}"] = lambda c=c: do_activate(c)
        steps[f"der{c}"] = lambda c=c: do_derive(c)
        steps[f"pr{c}"] = lambda c=c: do_project(c)
        steps[f"pb{c}"] = lambda c=c: do_pull_back(c)
        for g in range(3):
            steps[f"x{c}{g}"] = lambda c=c, g=g: keep(("dx", c, g), scatter_x(c, g, kept["c", c, g]))
            steps[f"y{c}{g}"] = lambda c=c, g=g: keep(
                ("d", c, g), kept.pop(("dx", c, g)) + scatter_y(c, g, kept.pop(("c", c, g)))
            )
        for g in range(2):
            steps[f"f{c}{g}"] = lambda c=c, g=g: keep(("f", c, g), gather_on(c, g, kept.pop(("e", c, g))))
    def token_terms():
        arrived([kept["px"], kept["py"]])
        for ref, at in ((xt.at[pl.ds(half_x, 320)], 0), (xt_far, ROWS)):
            hi, lo = split(ref[...])
            xth[pl.ds(0, 320), pl.ds(at, ROWS)] = hi
            xth[pl.ds(320, 320), pl.ds(at, ROWS)] = lo
        for c in range(2):
            dh[pl.ds(C * c, C), :] = ds_[c, pl.ds(0, C), :]
            dl[pl.ds(C * c, C), :] = ds_[c, pl.ds(C, C), :]
        dh[pl.ds(ROWS, ROWS), :], dl[pl.ds(ROWS, ROWS), :] = split(dy_far[...])

    def down_gradient():
        arrived([kept["ph"]])
        for ref, at in ((ht.at[pl.ds(half_h, 432)], 0), (ht_far, ROWS)):
            hi, lo = split(ref[...])
            hth[pl.ds(0, 432), pl.ds(at, ROWS)] = hi
            hth[pl.ds(432, 432), pl.ds(at, ROWS)] = lo
        gd_o[...] = dot3(hth[...], dh[...], dl[...], NN)

    def gate_up_gradients():
        arrived([kept["pg", 0], kept["pg", 1]])
        for i, o in enumerate((gg_o, gu_o)):
            for c in range(2):
                at = pl.ds(ROWS + C * c, C)
                bh[i, at, :], bl[i, at, :] = split(far[c, i].reshape(C, HP))
            o[...] = dot3(xth[...], bh[i], bl[i], NN)[:, :H]

    steps["tt"] = token_terms
    steps["gd"] = down_gradient
    steps["gw"] = gate_up_gradients
    for name in ORDER:
        steps[name]()

    arrived(kept["g", 0, 0] + kept["g", 0])
    out_o[...] = ring_sum(0, 0) + rx[0]
    arrived(kept["g", 1, 0])
    near = ring_sum(1, 0)
    if FAR_DIRECT:
        arrived(kept["g", 1, 1])
        gtok_o[...] = near + rf[0] + rf[1] + rf[2] + rf[3]
    else:
        arrived(kept["g", 1])
        gtok_o[...] = near + rx[1]
    for c in sent:
        c.wait_send()


def write(*refs):
    copies = []
    for i in range(5):
        src, dst, sems = refs[i], refs[5 + i], refs[10]
        n = PIECES[i]
        rows = src.shape[0] // n
        for k in range(n):
            at = pl.ds(rows * k, rows)
            copies.append(pltpu.make_async_copy(src.at[at], dst.at[at], sems.at[i, k]))
    for c in copies:
        c.start()
    for c in copies:
        c.wait()


def shards(tokens, cotangent, w_gate, w_up, w_down):
    v = pltpu.VMEM
    dma = pltpu.SemaphoreType.DMA
    cy = HP - CX
    scratch = [
        v((ROWS, W), F32), v((ROWS, W), F32), v((2, 2 * C, W), BF16), v((2, 2 * C, W), BF16),
        *[v((HP, W), F32)] * 3, *[v((HP, W), BF16)] * 6, *[v((W, HP), BF16)] * 6,
        v((2, 3, 2, 32, HP), F32), v((2, 3, 32, CX), F32), v((2, 3, 3, 8, CX), F32),
        v((2, 3, 3, 2, 8, cy), F32), v((2, 3, 8, cy), F32), v((2, 3, 32, CX), F32),
        v((2, 3, 2, 8, cy), F32), v((2, 3, 2, 32, HP), F32),
        v((W, ROWS), F32), v((320, ROWS), F32), v((ROWS, W), F32), v((HP, ROWS), F32), v((432, ROWS), F32),
        v((2, 2, 2, 32, HP), F32),
        v((640, 256), BF16), v((864, 256), BF16),
        v((2, 256, HP), BF16), v((2, 256, HP), BF16), v((256, W), BF16), v((256, W), BF16),
        v((2, 2, C, W), F32), v((2, 2, 3, 16, W), F32), v((2, 16, W), F32), v((2, 16, W), F32), v((4, 16, W), F32),
        dma((2, 7)), dma((2, 7)), dma((2, 3, 8)), dma((2, 3, 8)), dma((2, 2, 8)), dma((2, 2, 8)),
        dma((2, 2, 2, 4)), dma((2, 2, 2, 4)), dma((5,)), dma((5,)), dma((5,)),
    ]
    any_ = pl.BlockSpec(memory_space=pl.ANY)
    vmem = pl.BlockSpec(memory_space=pltpu.VMEM)
    hbm = pl.BlockSpec(memory_space=pltpu.HBM)
    shapes = [(16, W), (16, W), (320, H), (320, H), (432, W)]
    results = pl.pallas_call(
        kernel,
        out_shape=[v(s, F32) for s in shapes],
        in_specs=[hbm] * 5,
        out_specs=[vmem] * 5,
        scratch_shapes=scratch,
        compiler_params=pltpu.CompilerParams(
            collective_id=0, has_side_effects=True, vmem_limit_bytes=48 << 20
        ),
    )(*[pltpu.with_memory_space_constraint(a, pltpu.HBM) for a in (tokens, cotangent, w_gate.T, w_up.T, w_down)])
    results = [pltpu.with_memory_space_constraint(r, pltpu.VMEM) for r in results]
    out, gtok, gg, gu, gd = pl.pallas_call(
        write,
        out_shape=[jax.ShapeDtypeStruct(s, F32) for s in shapes],
        in_specs=[vmem] * 5,
        out_specs=[any_] * 5,
        scratch_shapes=[dma((5, max(PIECES)))],
    )(*results)
    return out, gtok, gg[None, None], gu[None, None], gd[None, None]


def solution(mesh):
    return jax.shard_map(
        shards,
        mesh=mesh,
        in_specs=(
            P(("rep", "hid"), "width"), P(("rep", "hid"), "width"),
            P("width", "hid"), P("width", "hid"), P("hid", "width"),
        ),
        out_specs=(
            P(("rep", "hid"), "width"), P(("rep", "hid"), "width"),
            P("width", "rep", None, "hid"), P("width", "rep", None, "hid"),
            P("hid", "rep", None, "width"),
        ),
        check_vma=False,
    )
```
